32 devices in a mesh: fsdp: 16 (over z, y, core), seq: 2 (over x).
Axes of the slice: x: 2, y: 2, z: 4, core: 2. Of those that a mesh axis runs over, the one named last changes fastest.
Arguments:
- img_in: bfloat16 [32, 1024, 1536], P('fsdp', 'seq'), may hold values from -6 to 6
- txt_in: bfloat16 [32, 162, 1536], P('fsdp', 'seq'), may hold values from -6 to 6
- cond: bfloat16 [32, 1536], P('fsdp'), may hold values from -6 to 6
- text_counts: int32 [32, 2], P('fsdp'), may hold values from 1 to 81, 154 in all within a row
- ada_w: bfloat16 [2, 1536, 9216], P(None, 'fsdp'), may hold values from -0.15625 to 0.15625
- qkv_w: bfloat16 [2, 1536, 4608], P(None, 'fsdp'), may hold values from -0.15625 to 0.15625
- proj_w: bfloat16 [2, 1536, 1536], P(None, 'fsdp'), may hold values from -0.625 to 0.625
- fc1_w: bfloat16 [2, 1536, 6144], P(None, 'fsdp'), may hold values from -0.15625 to 0.15625
- fc2_w: bfloat16 [2, 6144, 1536], P(None, 'fsdp'), may hold values from -0.078125 to 0.078125
- qk_gain: float32 [2, 128], replicated, may hold values from 1 to 2
- img_cot: bfloat16 [32, 1024, 1536], P('fsdp', 'seq'), may hold values from -6 to 6
- txt_cot: bfloat16 [32, 162, 1536], P('fsdp', 'seq'), may hold values from -6 to 6
Outputs:
- img_out: bfloat16 [32, 1024, 1536], P('fsdp', 'seq')
- txt_out: bfloat16 [32, 162, 1536], P('fsdp', 'seq')
- img_grad: float32 [32, 1024, 1536], P('fsdp', 'seq')
- txt_grad: float32 [32, 162, 1536], P('fsdp', 'seq')
- cond_grad: float32 [32, 1536], P('fsdp')
- ada_grad: float32 [2, 1536, 9216], P(None, ('fsdp', 'seq'))
- qkv_grad: float32 [2, 1536, 4608], P(None, ('fsdp', 'seq'))
- proj_grad: float32 [2, 1536, 1536], P(None, ('fsdp', 'seq'))
- fc1_grad: float32 [2, 1536, 6144], P(None, ('fsdp', 'seq'))
- fc2_grad: float32 [2, 6144, 1536], P(None, ('fsdp', 'seq'))
- gain_grad: float32 [2, 128], replicated
The draws below stay inside these ranges and needn't reach their ends.
Inputs may be any that keep to these rules, and one draw needn't show every extreme that they name: `text_counts`: row s gives how many live text tokens each of the 2 members of seq holds for sequence s, in its first slots; each row sums to 154.
All inputs are finite; a program needn't handle non-finite values.
Results may differ from the reference program's by a relative error of at most 0.014.
The reference program's roundings to bfloat16 on the way count: a program that leaves them out, or rounds other values in their place, can miss the bound.
Values may be sent and summed in bfloat16 or wider, within the bound.
A program may use at most 704 MiB of HBM per device.

```python
import math
from functools import partial
import jax
import jax.numpy as jnp
import numpy as np
from jax import lax

D = 1536
HEADS = 24
HEAD = 64
FF = 6144
IMG = 1024
TXT = 154
SEQS = 32
TXT_SLOTS = 81
TXT_ALL = 162
N_SEQ = 2


def block_levels(key, shape, cuts, low, high):
    def one(position, parts):
        draws = jax.random.uniform(jax.random.fold_in(jax.random.fold_in(key, 6), position), (parts,), jnp.float32, low / len(cuts), high / len(cuts))
        return jnp.repeat(jnp.exp(draws), shape[position] // parts).reshape((-1,) + (1,) * (len(shape) - position - 1))

    level = one(*cuts[0])
    for cut in cuts[1:]:
        level = level * one(*cut)
    return level


def split_up(amount, total, reach, slope):
    portions = [(1 << 20) // math.isqrt(grade ** slope) + 1 for grade in range(2, amount + 1)]
    rest, holding = total - reach - (amount - 1), [1] * (amount - 1)
    while rest > 0:
        movable = [i for i in range(amount - 1) if holding[i] < reach]
        whole, left = sum([portions[i] for i in movable]), rest
        for i in movable:
            more = min(reach - holding[i], max(1, left * portions[i] // whole), rest)
            holding[i] = holding[i] + more
            rest = rest - more
    return np.array([reach] + holding)


def uneven_parts(stream_key, number_of, total, limit, lean):
    if number_of == 2:
        one = jax.random.randint(stream_key, (), max(1, total - limit), min(limit, total - 1) + 1)
        return jnp.stack([one, total - one])
    tallies = jnp.asarray(split_up(number_of, total, limit, lean), jnp.int32)
    couples = (number_of - 1) // 2
    giver, receiver = tallies[1:1 + 2 * couples:2], tallies[2:2 + 2 * couples:2]
    margin = jnp.minimum(giver - 1, limit - receiver)
    moved = jax.random.randint(jax.random.fold_in(stream_key, 1), (couples,), 0, 1 << 20) % (margin + 1)
    tallies = tallies.at[1:1 + 2 * couples:2].set(giver - moved).at[2:2 + 2 * couples:2].set(receiver + moved)
    return tallies[jax.random.permutation(jax.random.fold_in(stream_key, 2), number_of)]


def gaussian(rng, extent, spread, bound, shards=(), kind=jnp.bfloat16):
    array = spread * jax.random.normal(rng, extent, jnp.float32)
    if shards:
        array = array * block_levels(rng, extent, shards, -0.22, 0.18)
    return jnp.clip(array, -bound, bound).astype(kind)


def setup_inputs(seed: int = 0) -> dict:
    keys = jax.random.split(jax.random.key(seed), 13)
    img_in = gaussian(keys[0], (SEQS, IMG, D), 1.0, 6.0, ((0, 16), (1, 2)))
    txt_in = gaussian(keys[1], (SEQS, TXT_ALL, D), 1.0, 6.0, ((0, 16), (1, 2)))
    cond = gaussian(keys[2], (SEQS, D), 1.0, 6.0, ((0, 16),))
    text_counts = jax.vmap(lambda own: uneven_parts(own, N_SEQ, TXT, TXT_SLOTS, 1))(jax.random.split(keys[3], SEQS)).reshape((SEQS, N_SEQ)).astype(jnp.int32)
    ada_w = gaussian(keys[4], (2, D, 6 * D), D ** -0.5, 0.15625, ((1, 16),))
    qkv_w = gaussian(keys[5], (2, D, 3 * D), D ** -0.5, 0.15625, ((1, 16),))
    proj_w = gaussian(keys[6], (2, D, D), (D // 16) ** -0.5, 0.625, ((1, 16),))
    fc1_w = gaussian(keys[7], (2, D, FF), D ** -0.5, 0.15625, ((1, 16),))
    fc2_w = gaussian(keys[8], (2, FF, D), FF ** -0.5, 0.078125, ((1, 16),))
    qk_gain = jnp.clip(jnp.exp(jax.random.uniform(keys[9], (2, 2 * HEAD), jnp.float32, math.log(1.0), math.log(2.0))), 1.0, 2.0)
    img_cot = gaussian(keys[10], (SEQS, IMG, D), 1.0, 6.0, ((0, 16), (1, 2)))
    txt_cot = gaussian(keys[11], (SEQS, TXT_ALL, D), 1.0, 6.0, ((0, 16), (1, 2)))
    return dict(img_in=img_in, txt_in=txt_in, cond=cond, text_counts=text_counts, ada_w=ada_w, qkv_w=qkv_w, proj_w=proj_w, fc1_w=fc1_w, fc2_w=fc2_w, qk_gain=qk_gain, img_cot=img_cot, txt_cot=txt_cot)


@jax.custom_vjp
def low(v):
    return lax.optimization_barrier(v.astype(jnp.bfloat16)).astype(jnp.float32)

@jax.custom_vjp
def low_back(v):
    return v

def low_keep(v):
    return (low(v), None)

def low_pass(kept, grad):
    return (grad,)

def back_keep(v):
    return (v, None)

def back_low(kept, grad):
    return (low(grad),)
low.defvjp(low_keep, low_pass)
low_back.defvjp(back_keep, back_low)

def product(left, right):
    return jnp.dot(left, right, precision=lax.Precision.HIGHEST, preferred_element_type=jnp.float32)

def layer_norm(values):
    average = lax.optimization_barrier(jnp.mean(values, axis=-1, keepdims=True))
    centred = values - average
    variance = lax.optimization_barrier(jnp.mean(centred * centred, axis=-1, keepdims=True))
    return centred * lax.rsqrt(variance + 1e-06)

def rms_heads(values, gain_vec):
    shaped = values.reshape(values.shape[:-1] + (HEADS, HEAD))
    square = lax.optimization_barrier(jnp.mean(shaped * shaped, axis=-1, keepdims=True))
    return (shaped * lax.rsqrt(square + 1e-06) * gain_vec).reshape(values.shape)

def one_sequence(weights, image_rows, text_rows, mod_rows, live_mask):
    qkv_w, proj_w, fc1_w, fc2_w, qk_gain = weights
    inputs = (image_rows, text_rows)
    pieces = []
    queries = []
    keys_all = []
    values_all = []
    for modality in range(2):
        shift_attn, scale_attn, gate_attn, shift_mlp, scale_mlp, gate_mlp = jnp.split(mod_rows[modality], 6)
        pieces.append((shift_mlp, scale_mlp, gate_attn, gate_mlp))
        normed_in = low(layer_norm(inputs[modality]) * (1.0 + scale_attn) + shift_attn)
        qkv_raw = low_back(product(normed_in, qkv_w[modality]))
        queries.append(low_back(low(rms_heads(qkv_raw[:, :D], qk_gain[modality, :HEAD]))))
        keys_all.append(low_back(low(rms_heads(qkv_raw[:, D:2 * D], qk_gain[modality, HEAD:]))))
        values_all.append(low(qkv_raw[:, 2 * D:]))
    length = IMG + TXT_ALL
    query_heads = jnp.concatenate(queries, axis=0).reshape(length, HEADS, HEAD)
    key_heads = jnp.concatenate(keys_all, axis=0).reshape(length, HEADS, HEAD)
    value_heads = jnp.concatenate(values_all, axis=0).reshape(length, HEADS, HEAD)
    scores = jnp.einsum('qhe,khe->hqk', query_heads, key_heads, precision=lax.Precision.HIGHEST) * HEAD ** (-0.5)
    scores = low_back(scores)
    keys_live = jnp.concatenate([jnp.ones((IMG,), jnp.float32), live_mask])
    scores = jnp.where(keys_live > 0.5, scores, -1000000000.0)
    probabilities = low(jax.nn.softmax(scores, axis=-1))
    attended = jnp.einsum('hqk,khe->qhe', probabilities, value_heads, precision=lax.Precision.HIGHEST)
    attended = low_back(low(attended.reshape(length, D)))
    outputs = []
    for modality in range(2):
        shift_mlp, scale_mlp, gate_attn, gate_mlp = pieces[modality]
        portion = attended[:IMG] if modality == 0 else attended[IMG:]
        branch = low_back(product(portion, proj_w[modality]))
        middle = inputs[modality] + gate_attn * branch
        normed_mid = low(layer_norm(middle) * (1.0 + scale_mlp) + shift_mlp)
        hidden = low_back(product(normed_mid, fc1_w[modality]))
        activated = low(jax.nn.gelu(hidden, approximate=True))
        mlp_out = low_back(product(activated, fc2_w[modality]))
        outputs.append(middle + gate_mlp * mlp_out)
    return (outputs[0], outputs[1] * live_mask[:, None])

def reference(img_in, txt_in, cond, text_counts, ada_w, qkv_w, proj_w, fc1_w, fc2_w, qk_gain, img_cot, txt_cot):
    slot_ids = jnp.arange(TXT_SLOTS, dtype=jnp.int32)
    live_mask = (slot_ids[None, None, :] < text_counts[:, :, None]).astype(jnp.float32).reshape(SEQS, TXT_ALL)
    params = (ada_w.astype(jnp.float32), qkv_w.astype(jnp.float32), proj_w.astype(jnp.float32), fc1_w.astype(jnp.float32), fc2_w.astype(jnp.float32), qk_gain.astype(jnp.float32))

    def forward(weights, image_all, text_all, cond_all):
        cond_act = low(jax.nn.silu(cond_all))
        modulation = low_back(jnp.einsum('sd,tdm->stm', cond_act, weights[0], precision=lax.Precision.HIGHEST))
        step_fn = jax.checkpoint(partial(one_sequence, weights[1:]))

        def scan_step(carry, items):
            return (carry, step_fn(*items))
        _, outputs = lax.scan(scan_step, jnp.zeros((), jnp.float32), (image_all, text_all, modulation, live_mask))
        return outputs
    primal, pull = jax.vjp(forward, params, img_in.astype(jnp.float32), txt_in.astype(jnp.float32), cond.astype(jnp.float32))
    weight_grads, img_grad, txt_grad, cond_grad = pull((img_cot.astype(jnp.float32), txt_cot.astype(jnp.float32)))
    return (primal[0].astype(jnp.bfloat16), primal[1].astype(jnp.bfloat16), img_grad, txt_grad, cond_grad, weight_grads[0], weight_grads[1], weight_grads[2], weight_grads[3], weight_grads[4], weight_grads[5])
```

```python
import math

import jax
import jax.numpy as jnp
from jax import lax
from jax.experimental import pallas as pl
from jax.experimental.pallas import tpu as pltpu
from jax.sharding import PartitionSpec as P

HEAD = 64
LANES = 128
BLOCK = 256
BF16 = jnp.bfloat16
F32 = jnp.float32
SCALE = HEAD**-0.5
SCALE2 = SCALE * math.log2(math.e)
VMEM_LIMIT = 56 * 1024 * 1024
NT = (((1,), (1,)), ((), ()))
NN = (((1,), (0,)), ((), ()))


def dot(left, right, dims=NN):
    return lax.dot_general(left, right, dims, preferred_element_type=F32)


def low_lanes():
    return lax.broadcasted_iota(jnp.int32, (1, LANES), 1) < HEAD


def head_mean(values):
    low = low_lanes()
    first = jnp.sum(jnp.where(low, values, 0.0), axis=-1, keepdims=True)
    second = jnp.sum(jnp.where(low, 0.0, values), axis=-1, keepdims=True)
    return jnp.where(low, first, second) * (1.0 / HEAD)


def rms(values):
    return lax.rsqrt(head_mean(values * values) + 1e-06)


def blocks_of(total, size):
    return [(start, min(size, total - start)) for start in range(0, total, size)]


def attend_kernel(rows, img_total, *refs):
    count = len(rows)
    raw, refs = refs[: 3 * count], refs[3 * count :]
    gain_ref, live_ref = refs[:2]
    out, refs = refs[2 : 2 + count], refs[2 + count :]
    norm_ref, q_s, k0_s, k1_s, v0_s, v1_s, o_s = refs
    low = low_lanes()
    offset = 0
    for i, size in enumerate(rows):
        text = offset >= img_total
        place = pl.ds(offset, size)
        gain = 2 if text else 0
        query, key, value = (raw[3 * i + part][0] for part in range(3))
        q_s[place, :] = (query * rms(query) * gain_ref[gain : gain + 1, :]).astype(BF16)
        key = key * rms(key) * gain_ref[gain + 1 : gain + 2, :]
        k0_s[place, :] = jnp.where(low, key, 0.0).astype(BF16)
        k1_s[place, :] = jnp.where(low, 0.0, key).astype(BF16)
        if text:
            live = live_ref[0, pl.ds(offset - img_total, size), :]
            value = value * live
        else:
            live = jnp.ones_like(value)
        v0_s[place, :] = jnp.where(low, value, live).astype(BF16)
        v1_s[place, :] = jnp.where(low, live, value).astype(BF16)
        offset += size

    def block(start, size):
        place = pl.ds(start, size)
        query = q_s[place, :]
        sums = []
        for key_ref, value_ref in ((k0_s, v0_s), (k1_s, v1_s)):
            weights = jnp.exp2(dot(query, key_ref[...], NT) * SCALE2).astype(BF16)
            sums.append(dot(weights, value_ref[...]))
        top = jnp.where(low, sums[0], sums[1])
        bottom = pltpu.roll(jnp.where(low, sums[1], sums[0]), HEAD, 1)
        o_s[place, :] = (top / bottom).astype(BF16)
        turned = jnp.log2(bottom).T
        norm_ref[0, 0, 0:8, place] = turned[0:8]
        norm_ref[0, 0, 8:16, place] = turned[HEAD : HEAD + 8]

    def step(i, carry):
        block(pl.multiple_of(i * BLOCK, BLOCK), BLOCK)
        return carry

    lax.fori_loop(0, img_total // BLOCK, step, 0)
    for start, size in blocks_of(offset - img_total, BLOCK):
        block(img_total + start, size)
    offset = 0
    for i, size in enumerate(rows):
        out[i][0] = o_s[pl.ds(offset, size), :]
        offset += size


def attend_back_kernel(rows, img_total, width, *refs):
    count = len(rows)
    raw, refs = refs[: 3 * count], refs[3 * count :]
    grad, refs = refs[:count], refs[count:]
    done, refs = refs[:count], refs[count:]
    norm_ref, gain_ref, live_ref = refs[:3]
    out, refs = refs[3 : 3 + count], refs[3 + count :]
    gain_out, q_s, k_s, v_s, kt_s, do_s, o_s, dq_s, dk_s, dv_s = refs
    low = low_lanes()
    pair = pl.program_id(1)
    offset = 0
    for i, size in enumerate(rows):
        text = offset >= img_total
        place = pl.ds(offset, size)
        gain = 2 if text else 0
        query, key, value = (raw[3 * i + part][0] for part in range(3))
        q_s[place, :] = (query * rms(query) * gain_ref[gain : gain + 1, :]).astype(BF16)
        key = (key * rms(key) * gain_ref[gain + 1 : gain + 2, :]).astype(BF16)
        k_s[place, :] = key
        v_s[place, :] = value.astype(BF16)
        do_s[place, :] = grad[i][0]
        o_s[place, :] = done[i][0]
        offset += size
    total = offset
    key_blocks = blocks_of(img_total, BLOCK) + [
        (img_total + start, size) for start, size in blocks_of(total - img_total, BLOCK)
    ]
    for start, size in key_blocks:
        key = k_s[pl.ds(start, size), :].astype(F32)
        if start >= img_total:
            key = key * live_ref[0, pl.ds(start - img_total, size), :]
        kt_s[:, pl.ds(start, size)] = key.T.astype(BF16)
    dk_s[...] = jnp.zeros_like(dk_s)
    dv_s[...] = jnp.zeros_like(dv_s)

    def block(start, size):
        place = pl.ds(start, size)
        query = q_s[place, :]
        grads = do_s[place, :]
        both = (grads.astype(F32) * o_s[place, :].astype(F32)).T
        turned = []
        for h in range(2):
            delta = jnp.sum(both[h * HEAD : (h + 1) * HEAD], axis=0, keepdims=True)
            norm = norm_ref[0, 0, 8 * h : 8 * h + 1, place]
            own = low if h == 0 else jnp.logical_not(low)
            query_h = jnp.where(own, query, jnp.zeros_like(query))
            grads_h = jnp.where(own, grads, jnp.zeros_like(grads))
            total_t = jnp.zeros((HEAD, size), F32)
            for key_start, key_size in key_blocks:
                keys = pl.ds(key_start, key_size)
                prob = jnp.exp2(dot(k_s[keys, :], query_h, NT) * SCALE2 - norm)
                prob_grad = dot(v_s[keys, :], grads_h, NT)
                score_grad = (prob * (prob_grad - delta)).astype(BF16)
                dv_s[keys, :] += dot(prob.astype(BF16), grads_h)
                dk_s[keys, :] += dot(score_grad, query_h)
                total_t += dot(kt_s[h * HEAD : (h + 1) * HEAD, keys], score_grad)
            turned.append(total_t)
        dq_s[place, :] = jnp.concatenate(turned, axis=0).T

    def step(i, carry):
        block(pl.multiple_of(i * BLOCK, BLOCK), BLOCK)
        return carry

    lax.fori_loop(0, img_total // BLOCK, step, 0)
    for start, size in blocks_of(total - img_total, BLOCK):
        block(img_total + start, size)

    gain_sums = [jnp.zeros((1, LANES), F32) for _ in range(4)]
    offset = 0
    for i, size in enumerate(rows):
        text = offset >= img_total
        place = pl.ds(offset, size)
        value_grad = dv_s[place, :]
        key_grad = dk_s[place, :]
        if text:
            live = live_ref[0, pl.ds(offset - img_total, size), :]
            value_grad = value_grad * live
            key_grad = key_grad * live
        for part, change in enumerate((dq_s[place, :], key_grad)):
            row = (2 if text else 0) + part
            change = (change * SCALE).astype(BF16).astype(F32)
            values = raw[3 * i + part][0]
            root = rms(values)
            unit = values * root
            gain_sums[row] += jnp.sum(change * unit, axis=0, keepdims=True)
            change = change * gain_ref[row : row + 1, :]
            change = root * (change - unit * head_mean(change * unit))
            column = pl.multiple_of(part * width + pair * LANES, LANES)
            out[i][0, :, pl.ds(column, LANES)] = change.astype(BF16)
        column = pl.multiple_of(2 * width + pair * LANES, LANES)
        out[i][0, :, pl.ds(column, LANES)] = value_grad.astype(BF16)
        offset += size
    for row in range(4):
        gain_out[0, 0, row : row + 1, :] = gain_sums[row]
    gain_out[0, 0, 4:8, :] = jnp.zeros((4, LANES), F32)


def raw_specs(rows, pairs):
    return [
        pl.BlockSpec((1, size, LANES), lambda s, p, part=part: (s, 0, part * pairs + p))
        for size in rows
        for part in range(3)
    ]


def head_specs(rows):
    return [pl.BlockSpec((1, size, LANES), lambda s, p: (s, 0, p)) for size in rows]


def attend(raw, gains, live, img_total):
    sequences, _, triple = raw[0].shape
    width = triple // 3
    pairs = width // LANES
    rows = [piece.shape[1] for piece in raw]
    total = sum(rows)

    def kernel(*refs):
        attend_kernel(rows, img_total, *refs)

    work = sequences * pairs * 2 * total * total
    outputs = pl.pallas_call(
        kernel,
        grid=(sequences, pairs),
        in_specs=raw_specs(rows, pairs)
        + [
            pl.BlockSpec((4, LANES), lambda s, p: (0, 0)),
            pl.BlockSpec((1, total - img_total, LANES), lambda s, p: (s, 0, 0)),
        ],
        out_specs=head_specs(rows) + [pl.BlockSpec((1, 1, 16, total), lambda s, p: (s, p, 0, 0))],
        out_shape=[jax.ShapeDtypeStruct((sequences, size, width), BF16) for size in rows]
        + [jax.ShapeDtypeStruct((sequences, pairs, 16, total), F32)],
        scratch_shapes=[pltpu.VMEM((total, LANES), BF16)] * 6,
        compiler_params=pltpu.CompilerParams(vmem_limit_bytes=VMEM_LIMIT),
        cost_estimate=pl.CostEstimate(
            flops=work * 4 * LANES, bytes_accessed=sequences * total * width * 14, transcendentals=work
        ),
        name="attend",
    )(*[piece for piece in raw for _ in range(3)], gains, live)
    return (outputs[:-1], outputs[-1])


def attend_back(raw, grads, done, norm, gains, live, img_total):
    sequences, _, triple = raw[0].shape
    width = triple // 3
    pairs = width // LANES
    rows = [piece.shape[1] for piece in raw]
    total = sum(rows)

    def kernel(*refs):
        attend_back_kernel(rows, img_total, width, *refs)

    work = sequences * pairs * 2 * total * total
    outputs = pl.pallas_call(
        kernel,
        grid=(sequences, pairs),
        in_specs=raw_specs(rows, pairs)
        + head_specs(rows)
        + head_specs(rows)
        + [
            pl.BlockSpec((1, 1, 16, total), lambda s, p: (s, p, 0, 0)),
            pl.BlockSpec((4, LANES), lambda s, p: (0, 0)),
            pl.BlockSpec((1, total - img_total, LANES), lambda s, p: (s, 0, 0)),
        ],
        out_specs=[pl.BlockSpec((1, size, triple), lambda s, p: (s, 0, 0)) for size in rows]
        + [pl.BlockSpec((1, 1, 8, LANES), lambda s, p: (s, p, 0, 0))],
        out_shape=[jax.ShapeDtypeStruct((sequences, size, triple), BF16) for size in rows]
        + [jax.ShapeDtypeStruct((sequences, pairs, 8, LANES), F32)],
        scratch_shapes=[pltpu.VMEM((total, LANES), BF16)] * 3
        + [pltpu.VMEM((LANES, total), BF16)]
        + [pltpu.VMEM((total, LANES), BF16)] * 2
        + [pltpu.VMEM((total, LANES), F32)] * 3,
        compiler_params=pltpu.CompilerParams(vmem_limit_bytes=VMEM_LIMIT),
        cost_estimate=pl.CostEstimate(
            flops=work * 10 * LANES, bytes_accessed=sequences * total * width * 22, transcendentals=work
        ),
        name="attend_back",
    )(*[piece for piece in raw for _ in range(3)], *grads, *done, norm, gains, live)
    return (outputs[:-1], outputs[-1])


def shift_seq(values, amount):
    members = lax.axis_size("seq")
    return lax.ppermute(values, "seq", [(i, (i + amount) % members) for i in range(members)])


def gather_seq(values):
    return [values] + [shift_seq(values, k) for k in range(1, lax.axis_size("seq"))]


def sum_seq(parts):
    total = parts[0]
    for k in range(1, len(parts)):
        total = total + shift_seq(parts[k].astype(BF16), -k).astype(F32)
    return total


def pick(values, index, axis):
    return lax.dynamic_index_in_dim(values, index, axis, keepdims=False)


def reduce_fsdp(values):
    size = lax.axis_size("fsdp")
    me = lax.axis_index("fsdp")
    terms = [values]
    bit = 1
    while bit < size:
        mine = (me // bit) % 2
        halves = [t.reshape((t.shape[0] // 2, 2) + t.shape[1:]) for t in terms]
        away = sum(pick(t, 1 - mine, 1).astype(F32) for t in halves).astype(BF16)
        swap = [(i, i ^ bit) for i in range(size)]
        came = lax.ppermute(away, "fsdp", swap)
        terms = [pick(t, mine, 1) for t in halves] + [came]
        bit *= 2
    return sum(t.astype(F32) for t in terms)[0]


def rows_to_members(values):
    members = lax.axis_size("seq")
    me = lax.axis_index("seq")
    blocks = values.reshape((members, values.shape[0] // members) + values.shape[1:])
    parts = [pick(blocks, me, 0)]
    for k in range(1, members):
        parts.append(shift_seq(pick(blocks, (me + k) % members, 0), k))
    return [pick(jnp.stack(parts), (me - i) % members, 0) for i in range(members)]


def statistics(values):
    average = jnp.mean(values, axis=-1, keepdims=True)
    centred = values - average
    return (average, lax.rsqrt(jnp.mean(centred * centred, axis=-1, keepdims=True) + 1e-06))


def norm_back(grad, unit, root):
    return root * (
        grad
        - jnp.mean(grad, axis=-1, keepdims=True)
        - unit * jnp.mean(grad * unit, axis=-1, keepdims=True)
    )


def times(left, right):
    return lax.dot_general(left, right, (((2,), (0,)), ((), ())), preferred_element_type=F32)


def times_t(left, right):
    return lax.dot_general(left, right, (((2,), (1,)), ((), ())), preferred_element_type=F32)


def outer(lefts, rights):
    total = 0.0
    for left, right in zip(lefts, rights):
        total = total + lax.dot_general(
            left, right, (((0, 1), (0, 1)), ((), ())), preferred_element_type=F32
        )
    return total.astype(BF16)


def gelu_tanh(values):
    return jax.nn.gelu(values, approximate=True)


def pad_rows(values, rows):
    return jnp.pad(values, ((0, 0), (0, rows - values.shape[1]), (0, 0)))


def body(
    img_in, txt_in, cond, text_counts, ada_w, qkv_w, proj_w, fc1_w, fc2_w, qk_gain, img_cot, txt_cot
):
    members = lax.axis_size("seq")
    member = lax.axis_index("seq")
    shards = lax.axis_size("fsdp")
    sequences, img_local, width = img_in.shape
    slots = txt_in.shape[1]
    padded = -(-slots // 16) * 16
    img_total = members * img_local
    head_width = width // members
    head_padded = -(-head_width // LANES) * LANES
    hidden_width = fc1_w.shape[2]
    shard_rows = ada_w.shape[1]

    own_qkv = pick(qkv_w.reshape(2, shard_rows, 3, members, head_width), member, 3)
    if head_padded > head_width:
        own_qkv = jnp.pad(own_qkv, ((0, 0), (0, 0), (0, 0), (0, head_padded - head_width)))
    own_qkv = own_qkv.reshape(2, shard_rows, 3 * head_padded)
    unit_rows = hidden_width // (shards * members)
    own_fc1 = pick(fc1_w.reshape(2, shard_rows, shards, members, unit_rows), member, 3)
    own_fc1 = own_fc1.reshape(2, shard_rows, shards * unit_rows)
    own_fc2 = pick(fc2_w.reshape(2, members, unit_rows, width), member, 1)
    w_qkv = lax.all_gather(own_qkv, "fsdp", axis=1, tiled=True)
    w_proj = lax.all_gather(proj_w, "fsdp", axis=1, tiled=True)
    w_fc1 = lax.all_gather(own_fc1, "fsdp", axis=1, tiled=True)
    w_fc2 = lax.all_gather(own_fc2, "fsdp", axis=1, tiled=True)

    cond_act = jax.nn.silu(cond.astype(F32)).astype(BF16)
    cond_cols = lax.all_to_all(
        cond_act.reshape(sequences, shards, shard_rows), "fsdp", split_axis=1, concat_axis=0, tiled=True
    ).reshape(shards * sequences, shard_rows)
    mod_width = ada_w.shape[2]
    share = mod_width // members
    own_ada = lax.dynamic_slice_in_dim(ada_w, member * share, share, 2)
    mod_part = jnp.einsum("sd,tdm->stm", cond_cols, own_ada, preferred_element_type=F32)
    mod_part = mod_part.reshape(shards, sequences, 2, share)
    mod_sum = jnp.sum(
        lax.all_to_all(mod_part, "fsdp", split_axis=0, concat_axis=0, tiled=True), axis=0
    )
    mod_shares = jnp.stack(gather_seq(mod_sum))
    modulation = jnp.concatenate(
        [pick(mod_shares, (member - i) % members, 0) for i in range(members)], axis=-1
    )

    counts = jnp.stack([pick(text_counts, (member - k) % members, 1) for k in range(members)], axis=1)
    slot_ids = lax.broadcasted_iota(jnp.int32, (sequences, members, padded), 2)
    live = (slot_ids < counts[:, :, None]).astype(F32)
    text_rows = live[:, 0, :, None]
    live_lanes = jnp.broadcast_to(
        live.reshape(sequences, members * padded, 1), (sequences, members * padded, LANES)
    )
    gains = jnp.tile(qk_gain.reshape(4, HEAD), (1, 2))

    inputs = (img_in.astype(F32), pad_rows(txt_in, padded).astype(F32))
    out_grads = (img_cot.astype(F32), pad_rows(txt_cot, padded).astype(F32) * text_rows)
    pieces = [
        [piece[:, None, :] for piece in jnp.split(modulation[:, t], 6, axis=-1)] for t in range(2)
    ]

    normed_in, in_stats = [], []
    for t in range(2):
        average, root = statistics(inputs[t])
        in_stats.append((average, root))
        shift, scale = pieces[t][0], pieces[t][1]
        normed = (((inputs[t] - average) * root) * (1.0 + scale) + shift).astype(BF16)
        normed_in.append(gather_seq(normed))
    raw = [times(normed_in[t][k], w_qkv[t]) for t in range(2) for k in range(members)]
    attended, norm = attend(raw, gains, live_lanes, img_total)
    own_attended = []
    for t in range(2):
        parts = attended[t * members : (t + 1) * members]
        parts = [parts[0]] + [shift_seq(parts[k], -k) for k in range(1, members)]
        parts = [part[..., :head_width] for part in parts]
        own_attended.append(jnp.roll(jnp.concatenate(parts, axis=-1), member * head_width, axis=-1))

    middle, branch, mid_stats, normed_mid, mlp_grad = [], [], [], [], []
    for t in range(2):
        gate = pieces[t][2]
        branch.append(times(own_attended[t], w_proj[t]))
        middle.append(inputs[t] + gate * branch[t])
        average, root = statistics(middle[t])
        mid_stats.append((average, root))
        shift, scale = pieces[t][3], pieces[t][4]
        normed = (((middle[t] - average) * root) * (1.0 + scale) + shift).astype(BF16)
        normed_mid.append(gather_seq(normed))
        mlp_grad.append(gather_seq((pieces[t][5] * out_grads[t]).astype(BF16)))
    outs, mid_grad, fc1_sum, fc2_sum, gate_mlp_grad = [], [], [], [], []
    for t in range(2):
        hidden = [times(normed_mid[t][k], w_fc1[t]) for k in range(members)]
        active = [gelu_tanh(h).astype(BF16) for h in hidden]
        hidden_grad = []
        for k in range(members):
            active_grad = times_t(mlp_grad[t][k], w_fc2[t])
            hidden_grad.append(jax.vjp(gelu_tanh, hidden[k])[1](active_grad)[0].astype(BF16))
        mid_grad.append(sum_seq([times_t(hidden_grad[k], w_fc1[t]) for k in range(members)]))
        mlp_out = sum_seq([times(active[k], w_fc2[t]) for k in range(members)])
        result = middle[t] + pieces[t][5] * mlp_out
        outs.append(result)
        gate_mlp_grad.append(jnp.sum(out_grads[t] * mlp_out, axis=1))
        fc2_sum.append(
            reduce_fsdp(outer(active, mlp_grad[t]).reshape(shards, unit_rows, width))
        )
        fc1_sum.append(
            reduce_fsdp(outer(normed_mid[t], hidden_grad).reshape(shards, shard_rows, -1))
        )
    img_out = outs[0].astype(BF16)
    txt_out = (outs[1] * text_rows).astype(BF16)[:, :slots]

    middle_grad, head_grads, proj_sum, mod_grads = [], [], [], []
    for t in range(2):
        average, root = mid_stats[t]
        unit = (middle[t] - average) * root
        scale_mlp_grad = jnp.sum(mid_grad[t] * unit, axis=1)
        shift_mlp_grad = jnp.sum(mid_grad[t], axis=1)
        total = out_grads[t] + norm_back(mid_grad[t] * (1.0 + pieces[t][4]), unit, root)
        middle_grad.append(total)
        gate_attn_grad = jnp.sum(total * branch[t], axis=1)
        mod_grads.append([gate_attn_grad, shift_mlp_grad, scale_mlp_grad, gate_mlp_grad[t]])
        branch_grad = (pieces[t][2] * total).astype(BF16)
        attended_grad = times_t(branch_grad, w_proj[t]).astype(BF16)
        attended_grad = jnp.roll(attended_grad, -member * head_width, axis=-1)
        for k in range(members):
            part = attended_grad[..., k * head_width : (k + 1) * head_width]
            if head_padded > head_width:
                part = jnp.pad(part, ((0, 0), (0, 0), (0, head_padded - head_width)))
            head_grads.append(shift_seq(part, k) if k else part)
        proj_sum.append(
            reduce_fsdp(
                outer([own_attended[t]], [branch_grad]).reshape(shards, shard_rows, width)
            )
        )
    raw_grads, gain_parts = attend_back(
        raw, head_grads, attended, norm, gains, live_lanes, img_total
    )
    raw_grads = [raw_grads[t * members : (t + 1) * members] for t in range(2)]
    qkv_sum, in_grads = [], []
    for t in range(2):
        qkv_sum.append(
            reduce_fsdp(
                outer(normed_in[t], raw_grads[t]).reshape(shards, shard_rows, 3 * head_padded)
            )
        )
        in_grad = sum_seq([times_t(raw_grads[t][k], w_qkv[t]) for k in range(members)])
        average, root = in_stats[t]
        unit = (inputs[t] - average) * root
        scale_attn_grad = jnp.sum(in_grad * unit, axis=1)
        shift_attn_grad = jnp.sum(in_grad, axis=1)
        in_grads.append(middle_grad[t] + norm_back(in_grad * (1.0 + pieces[t][1]), unit, root))
        mod_grads[t] = jnp.concatenate([shift_attn_grad, scale_attn_grad] + mod_grads[t], axis=-1)
    img_grad, txt_grad = in_grads[0], in_grads[1][:, :slots]

    fc2_grad = jnp.stack(fc2_sum)
    fc1_grad, qkv_grad, proj_grad = [], [], []
    for t in range(2):
        parts = rows_to_members(fc1_sum[t])
        parts = [part.reshape(part.shape[0], shards, 1, unit_rows) for part in parts]
        fc1_grad.append(jnp.concatenate(parts, axis=2).reshape(-1, hidden_width))
        parts = rows_to_members(qkv_sum[t])
        parts = [part.reshape(-1, 3, 1, head_padded)[..., :head_width] for part in parts]
        qkv_grad.append(jnp.concatenate(parts, axis=2).reshape(-1, 3 * width))
        blocks = proj_sum[t].reshape(members, -1, width)
        total = pick(blocks, member, 0)
        for k in range(1, members):
            total = total + shift_seq(pick(blocks, (member + k) % members, 0), k)
        proj_grad.append(total)
    fc1_grad, qkv_grad, proj_grad = jnp.stack(fc1_grad), jnp.stack(qkv_grad), jnp.stack(proj_grad)

    gain_own = jnp.sum(gain_parts, axis=(0, 1))[:4]
    gain_own = (gain_own[:, :HEAD] + gain_own[:, HEAD:]).reshape(-1)
    mod_own = jnp.stack(mod_grads, axis=1).reshape(-1)
    both = jnp.concatenate([mod_own, gain_own])
    both = sum(gather_seq(both))
    mod_count = mod_own.shape[0]
    gain_high = both[mod_count:].astype(BF16)
    gain_low = (both[mod_count:] - gain_high.astype(F32)).astype(BF16)
    packed = jnp.concatenate([both[:mod_count].astype(BF16), gain_high, gain_low])[None]
    every = lax.all_gather(packed, "fsdp", axis=0, tiled=True)
    every_mod = every[:, :mod_count].reshape(shards * sequences, 2, mod_width)
    gain_grad = jnp.sum(every[:, mod_count:].astype(F32), axis=0).reshape(2, 2, 2 * HEAD).sum(axis=0)
    out_rows = width // (shards * members)
    own_cols = lax.dynamic_slice_in_dim(cond_cols, member * out_rows, out_rows, 1)
    ada_grad = jnp.einsum("sr,stm->trm", own_cols, every_mod, preferred_element_type=F32)
    cond_part = jnp.einsum("stm,tdm->sd", every_mod, ada_w, preferred_element_type=F32)
    cond_full = lax.all_to_all(cond_part, "fsdp", split_axis=0, concat_axis=1, tiled=True)
    cond_grad = jax.vjp(jax.nn.silu, cond.astype(F32))[1](cond_full)[0]
    return (
        img_out,
        txt_out,
        img_grad,
        txt_grad,
        cond_grad,
        ada_grad,
        qkv_grad,
        proj_grad,
        fc1_grad,
        fc2_grad,
        gain_grad,
    )


def solution(mesh):
    tokens, rows = P("fsdp", "seq", None), P("fsdp", None)
    weight, weight_grad = P(None, "fsdp", None), P(None, ("fsdp", "seq"), None)
    in_specs = (tokens, tokens, rows, rows) + (weight,) * 5 + (P(), tokens, tokens)
    out_specs = (tokens,) * 4 + (rows,) + (weight_grad,) * 5 + (P(),)
    return jax.shard_map(body, mesh=mesh, in_specs=in_specs, out_specs=out_specs, check_vma=False)
```

```python
import math

import jax
import jax.numpy as jnp
from jax import lax
from jax.experimental import pallas as pl
from jax.experimental.pallas import tpu as pltpu
from jax.sharding import PartitionSpec as P

HEAD = 64
LANES = 128
BLOCK = 512
BF16 = jnp.bfloat16
F32 = jnp.float32
SCALE = HEAD**-0.5
SCALE2 = SCALE * math.log2(math.e)
VMEM_LIMIT = 56 * 1024 * 1024
NT = (((1,), (1,)), ((), ()))
NN = (((1,), (0,)), ((), ()))


def dot(left, right, dims=NN):
    return lax.dot_general(left, right, dims, preferred_element_type=F32)


def low_lanes():
    return lax.broadcasted_iota(jnp.int32, (1, LANES), 1) < HEAD


def head_mean(values):
    low = low_lanes()
    first = jnp.sum(jnp.where(low, values, 0.0), axis=-1, keepdims=True)
    second = jnp.sum(jnp.where(low, 0.0, values), axis=-1, keepdims=True)
    return jnp.where(low, first, second) * (1.0 / HEAD)


def rms(values):
    return lax.rsqrt(head_mean(values * values) + 1e-06)


def blocks_of(total, size):
    return [(start, min(size, total - start)) for start in range(0, total, size)]


def attend_kernel(rows, img_total, *refs):
    count = len(rows)
    raw, refs = refs[: 3 * count], refs[3 * count :]
    gain_ref, live_ref = refs[:2]
    out, refs = refs[2 : 2 + count], refs[2 + count :]
    norm_ref, q_s, k0_s, k1_s, v0_s, v1_s, o_s = refs
    low = low_lanes()
    offset = 0
    for i, size in enumerate(rows):
        text = offset >= img_total
        place = pl.ds(offset, size)
        gain = 2 if text else 0
        query, key, value = (raw[3 * i + part][0] for part in range(3))
        q_s[place, :] = (query * rms(query) * gain_ref[gain : gain + 1, :]).astype(BF16)
        key = key * rms(key) * gain_ref[gain + 1 : gain + 2, :]
        k0_s[place, :] = jnp.where(low, key, 0.0).astype(BF16)
        k1_s[place, :] = jnp.where(low, 0.0, key).astype(BF16)
        if text:
            live = live_ref[0, pl.ds(offset - img_total, size), :]
            value = value * live
        else:
            live = jnp.ones_like(value)
        v0_s[place, :] = jnp.where(low, value, live).astype(BF16)
        v1_s[place, :] = jnp.where(low, live, value).astype(BF16)
        offset += size

    def block(start, size):
        place = pl.ds(start, size)
        query = q_s[place, :]
        sums = []
        for key_ref, value_ref in ((k0_s, v0_s), (k1_s, v1_s)):
            weights = jnp.exp2(dot(query, key_ref[...], NT) * SCALE2).astype(BF16)
            sums.append(dot(weights, value_ref[...]))
        top = jnp.where(low, sums[0], sums[1])
        bottom = pltpu.roll(jnp.where(low, sums[1], sums[0]), HEAD, 1)
        o_s[place, :] = (top / bottom).astype(BF16)
        turned = jnp.log2(bottom).T
        norm_ref[0, 0, 0:8, place] = turned[0:8]
        norm_ref[0, 0, 8:16, place] = turned[HEAD : HEAD + 8]

    def step(i, carry):
        block(pl.multiple_of(i * BLOCK, BLOCK), BLOCK)
        return carry

    lax.fori_loop(0, img_total // BLOCK, step, 0)
    for start, size in blocks_of(offset - img_total, BLOCK):
        block(img_total + start, size)
    offset = 0
    for i, size in enumerate(rows):
        out[i][0] = o_s[pl.ds(offset, size), :]
        offset += size


def attend_back_kernel(rows, img_total, width, *refs):
    count = len(rows)
    raw, refs = refs[: 3 * count], refs[3 * count :]
    grad, refs = refs[:count], refs[count:]
    done, refs = refs[:count], refs[count:]
    norm_ref, gain_ref, live_ref = refs[:3]
    out, refs = refs[3 : 3 + count], refs[3 + count :]
    gain_out, q_s, k_s, v_s, kt_s, do_s, o_s, dq_s, dk_s, dv_s = refs
    low = low_lanes()
    pair = pl.program_id(0)
    offset = 0
    for i, size in enumerate(rows):
        text = offset >= img_total
        place = pl.ds(offset, size)
        gain = 2 if text else 0
        query, key, value = (raw[3 * i + part][0] for part in range(3))
        q_s[place, :] = (query * rms(query) * gain_ref[gain : gain + 1, :]).astype(BF16)
        key = (key * rms(key) * gain_ref[gain + 1 : gain + 2, :]).astype(BF16)
        k_s[place, :] = key
        v_s[place, :] = value.astype(BF16)
        do_s[place, :] = grad[i][0]
        o_s[place, :] = done[i][0]
        offset += size
    total = offset
    key_blocks = blocks_of(img_total, BLOCK) + [
        (img_total + start, size) for start, size in blocks_of(total - img_total, BLOCK)
    ]
    for start, size in key_blocks:
        key = k_s[pl.ds(start, size), :].astype(F32)
        if start >= img_total:
            key = key * live_ref[0, pl.ds(start - img_total, size), :]
        kt_s[:, pl.ds(start, size)] = key.T.astype(BF16)
    dk_s[...] = jnp.zeros_like(dk_s)
    dv_s[...] = jnp.zeros_like(dv_s)

    def block(start, size):
        place = pl.ds(start, size)
        query = q_s[place, :]
        grads = do_s[place, :]
        both = (grads.astype(F32) * o_s[place, :].astype(F32)).T
        side = []
        for h in range(2):
            delta = jnp.sum(both[h * HEAD : (h + 1) * HEAD], axis=0, keepdims=True)
            norm = norm_ref[0, 0, 8 * h : 8 * h + 1, place]
            own = low if h == 0 else jnp.logical_not(low)
            query_h = jnp.where(own, query, jnp.zeros_like(query))
            grads_h = jnp.where(own, grads, jnp.zeros_like(grads))
            side.append((delta, norm, query_h, grads_h))
        probs, changes = [], []
        for delta, norm, query_h, grads_h in side:
            prob = jnp.exp2(dot(k_s[...], query_h, NT) * SCALE2 - norm)
            prob_grad = dot(v_s[...], grads_h, NT)
            changes.append((prob * (prob_grad - delta)).astype(BF16))
            probs.append(prob.astype(BF16))
        dv_s[...] += dot(probs[0], side[0][3]) + dot(probs[1], side[1][3])
        dk_s[...] += dot(changes[0], side[0][2]) + dot(changes[1], side[1][2])
        turned = [dot(kt_s[h * HEAD : (h + 1) * HEAD, :], changes[h]) for h in range(2)]
        dq_s[place, :] = jnp.concatenate(turned, axis=0).T

    def step(i, carry):
        block(pl.multiple_of(i * BLOCK, BLOCK), BLOCK)
        return carry

    lax.fori_loop(0, img_total // BLOCK, step, 0)
    for start, size in blocks_of(total - img_total, BLOCK):
        block(img_total + start, size)

    gain_sums = [jnp.zeros((1, LANES), F32) for _ in range(4)]
    offset = 0
    for i, size in enumerate(rows):
        text = offset >= img_total
        place = pl.ds(offset, size)
        value_grad = dv_s[place, :]
        key_grad = dk_s[place, :]
        if text:
            live = live_ref[0, pl.ds(offset - img_total, size), :]
            value_grad = value_grad * live
            key_grad = key_grad * live
        for part, change in enumerate((dq_s[place, :], key_grad)):
            row = (2 if text else 0) + part
            change = (change * SCALE).astype(BF16).astype(F32)
            values = raw[3 * i + part][0]
            root = rms(values)
            unit = values * root
            gain_sums[row] += jnp.sum(change * unit, axis=0, keepdims=True)
            change = change * gain_ref[row : row + 1, :]
            change = root * (change - unit * head_mean(change * unit))
            column = pl.multiple_of(part * width + pair * LANES, LANES)
            out[i][0, :, pl.ds(column, LANES)] = change.astype(BF16)
        column = pl.multiple_of(2 * width + pair * LANES, LANES)
        out[i][0, :, pl.ds(column, LANES)] = value_grad.astype(BF16)
        offset += size
    for row in range(4):
        gain_out[0, row : row + 1, :] = gain_sums[row]
    gain_out[0, 4:8, :] = jnp.zeros((4, LANES), F32)


def cost(flops, bytes_accessed, transcendentals=0):
    return pl.CostEstimate(
        flops=flops, bytes_accessed=bytes_accessed, transcendentals=transcendentals
    )


PARAMS = pltpu.CompilerParams(vmem_limit_bytes=VMEM_LIMIT)


def raw_specs(raw, group, count):
    return [
        pl.BlockSpec(
            (1, array.shape[1], LANES),
            lambda p, sel=sel, part=part: (sel, 0, (group * 3 + part) * count + p),
        )
        for array, sel in raw
        for part in range(3)
    ]


def rows_of(pieces):
    return [array.shape[1] for array, _ in pieces]


def attend(raw, gains, live, sequence, img_total, groups):
    width = raw[0][0].shape[2] // 3
    pairs = width // LANES
    count = pairs // groups
    rows = rows_of(raw)
    total = sum(rows)

    def kernel(*refs):
        attend_kernel(rows, img_total, *refs)

    work = pairs * 2 * total * total
    outputs = pl.pallas_call(
        kernel,
        grid=(pairs,),
        in_specs=[
            pl.BlockSpec(
                (1, array.shape[1], LANES),
                lambda p, sel=sel, part=part: (
                    sel,
                    0,
                    (p // count * 3 + part) * count + p % count,
                ),
            )
            for array, sel in raw
            for part in range(3)
        ]
        + [
            pl.BlockSpec((4, LANES), lambda p: (0, 0)),
            pl.BlockSpec((1, total - img_total, LANES), lambda p: (sequence, 0, 0)),
        ],
        out_specs=[pl.BlockSpec((1, size, LANES), lambda p: (0, 0, p)) for size in rows]
        + [pl.BlockSpec((1, 1, 16, total), lambda p: (0, p, 0, 0))],
        out_shape=[jax.ShapeDtypeStruct((1, size, width), BF16) for size in rows]
        + [jax.ShapeDtypeStruct((1, pairs, 16, total), F32)],
        scratch_shapes=[pltpu.VMEM((total, LANES), BF16)] * 6,
        compiler_params=PARAMS,
        cost_estimate=cost(work * 4 * LANES, total * width * 14, work),
        name="attend",
    )(*[array for array, _ in raw for _ in range(3)], gains, live)
    return (list(outputs[:-1]), outputs[-1])


def attend_back(raw, grads, done, norm, gains, live, sequence, img_total, groups, group, before):
    triple = raw[0][0].shape[2]
    width = triple // 3
    pairs = width // LANES
    count = pairs // groups
    rows = rows_of(raw)
    total = sum(rows)
    pieces = len(rows)

    def kernel(*refs):
        if before is not None:
            refs = refs[pieces:]
        attend_back_kernel(rows, img_total, count * LANES, *refs)

    head_specs = [
        pl.BlockSpec((1, size, LANES), lambda p: (0, 0, group * count + p)) for size in rows
    ]
    in_specs = (
        raw_specs(raw, group, count)
        + head_specs
        + head_specs
        + [
            pl.BlockSpec((1, 1, 16, total), lambda p: (0, group * count + p, 0, 0)),
            pl.BlockSpec((4, LANES), lambda p: (0, 0)),
            pl.BlockSpec((1, total - img_total, LANES), lambda p: (sequence, 0, 0)),
        ]
    )
    operands = [array for array, _ in raw for _ in range(3)]
    operands += [*grads, *done, norm, gains, live]
    aliases = {}
    if before is not None:
        in_specs = [pl.BlockSpec(memory_space=pl.ANY)] * pieces + in_specs
        operands = list(before) + operands
        aliases = {i: i for i in range(pieces)}
    work = count * 2 * total * total
    outputs = pl.pallas_call(
        kernel,
        grid=(count,),
        in_specs=in_specs,
        out_specs=[
            pl.BlockSpec((1, size, 3 * count * LANES), lambda p: (0, 0, group)) for size in rows
        ]
        + [pl.BlockSpec((1, 8, LANES), lambda p: (p, 0, 0))],
        out_shape=[jax.ShapeDtypeStruct((1, size, triple), BF16) for size in rows]
        + [jax.ShapeDtypeStruct((count, 8, LANES), F32)],
        scratch_shapes=[pltpu.VMEM((total, LANES), BF16)] * 3
        + [pltpu.VMEM((LANES, total), BF16)]
        + [pltpu.VMEM((total, LANES), BF16)] * 2
        + [pltpu.VMEM((total, LANES), F32)] * 3,
        compiler_params=PARAMS,
        input_output_aliases=aliases,
        cost_estimate=cost(work * 10 * LANES, total * count * LANES * 22, work),
        name="attend_back",
    )(*operands)
    return (list(outputs[:-1]), outputs[-1])


def tile_of(extent):
    for size in (1024, 768, 512, 384, 256, 128):
        if extent % size == 0:
            return size
    return extent


def hidden_back(hidden, grads, weight, modality):
    width = weight.shape[2]
    units = weight.shape[1]
    tile = tile_of(units)
    rows = rows_of(hidden)
    count = len(rows)

    def kernel(*refs):
        weight_ref = refs[2 * count]
        for i in range(count):
            value = refs[i][0]
            grad = dot(refs[count + i][0], weight_ref[0], NT)
            square = value * value
            slope = math.sqrt(2 / math.pi)
            bent = jnp.tanh(value * (slope + (slope * 0.044715) * square))
            half = 0.5 * value
            rise = 0.5 + 0.5 * bent
            refs[2 * count + 1 + i][0] = (half + half * bent).astype(BF16)
            rise = rise + half * (1.0 - bent * bent) * (slope + (3 * slope * 0.044715) * square)
            refs[3 * count + 1 + i][0] = (grad * rise).astype(BF16)

    total = sum(rows)
    outputs = pl.pallas_call(
        kernel,
        grid=(units // tile,),
        in_specs=[
            pl.BlockSpec((1, size, tile), lambda j, sel=sel: (sel, 0, j))
            for (_, sel), size in zip(hidden, rows)
        ]
        + [
            pl.BlockSpec((1, size, width), lambda j, sel=sel: (sel, 0, 0))
            for (_, sel), size in zip(grads, rows)
        ]
        + [pl.BlockSpec((1, tile, width), lambda j: (modality, j, 0))],
        out_specs=[pl.BlockSpec((1, size, tile), lambda j: (0, 0, j)) for size in rows] * 2,
        out_shape=[jax.ShapeDtypeStruct((1, size, units), BF16) for size in rows] * 2,
        compiler_params=PARAMS,
        cost_estimate=cost(
            2 * total * width * units, total * (2 * width + 8 * units) + 2 * units * width, total * units
        ),
        name="hidden_back",
    )(*[a for a, _ in hidden], *[a for a, _ in grads], weight)
    return (list(outputs[:count]), list(outputs[count:]))


def weight_sum(lefts, rights, blocks, bit=None, before=None, place=0, places=1):
    rows = lefts[0][0].shape[2]
    columns = rights[0][0].shape[2]
    block = rows // blocks
    row_tile = max(size for size in (768, 512, 384, rows) if rows % size == 0 and size % (2 * block) == 0)
    tile = tile_of(columns)
    sizes = rows_of(lefts)
    count = len(sizes)
    run = row_tile // block

    def kernel(*refs):
        bit_ref, refs = refs[0], refs[len(first) :]
        total = None
        for i in range(count):
            part = lax.dot_general(
                refs[i][0], refs[count + i][0], (((0,), (0,)), ((), ())), preferred_element_type=F32
            )
            total = part if total is None else total + part
        if bit is None:
            for j in range(run):
                refs[2 * count][j, 0] = total[j * block : (j + 1) * block].astype(BF16)
        else:
            keep_ref, away_ref = refs[2 * count :]
            odd = bit_ref[0] == 1
            for j in range(run // 2):
                even_rows = total[2 * j * block : (2 * j + 1) * block]
                odd_rows = total[(2 * j + 1) * block : (2 * j + 2) * block]
                keep_ref[j] = jnp.where(odd, odd_rows, even_rows).astype(BF16)
                away_ref[j] = jnp.where(odd, even_rows, odd_rows).astype(BF16)

    total = sum(sizes)
    if bit is None:
        out_shape = jax.ShapeDtypeStruct((blocks, places, block, columns), BF16)
        out_specs = pl.BlockSpec((run, 1, block, tile), lambda i, j: (i, place, 0, j))
    else:
        out_shape = [jax.ShapeDtypeStruct((blocks // 2, block, columns), BF16)] * 2
        out_specs = [pl.BlockSpec((run // 2, block, tile), lambda i, j: (i, 0, j))] * 2
    first_specs, first = [], []
    if bit is not None:
        first_specs, first = [pl.BlockSpec(memory_space=pltpu.SMEM)], [bit]
    elif before is not None:
        first_specs, first = [pl.BlockSpec(memory_space=pl.ANY)], [before]
    return pl.pallas_call(
        kernel,
        grid=(rows // row_tile, columns // tile),
        in_specs=first_specs
        + [
            pl.BlockSpec((1, size, row_tile), lambda i, j, sel=sel: (sel, 0, i))
            for (_, sel), size in zip(lefts, sizes)
        ]
        + [
            pl.BlockSpec((1, size, tile), lambda i, j, sel=sel: (sel, 0, j))
            for (_, sel), size in zip(rights, sizes)
        ],
        out_specs=out_specs,
        out_shape=out_shape,
        compiler_params=PARAMS,
        input_output_aliases={} if before is None else {0: 0},
        cost_estimate=cost(
            2 * total * rows * columns, 2 * (total * (rows + columns) + rows * columns)
        ),
        name="weight_sum",
    )(*first, *[a for a, _ in lefts], *[a for a, _ in rights])


def pick_heads(weight, other, member, members, groups, group_width):
    rows, columns = weight.shape
    width = columns // 3
    head_width = width // members
    size = lambda group: min(group_width, head_width - group * group_width)

    def kernel(member_ref, in_ref, other_ref, out_ref):
        for m in range(members):

            @pl.when(member_ref[0] == m)
            def _():
                for group in range(groups):
                    for part in range(3):
                        start = part * width + m * head_width + group * group_width
                        piece = in_ref[:, start : start + size(group)]
                        if size(group) < group_width:
                            blank = jnp.zeros((rows, group_width - size(group)), piece.dtype)
                            piece = jnp.concatenate([piece, blank], axis=1)
                        place = (group * 3 + part) * group_width
                        out_ref[:, place : place + group_width] = piece

        out_ref[:, 3 * groups * group_width :] = other_ref[...]

    total = 3 * groups * group_width + other.shape[1]
    return pl.pallas_call(
        kernel,
        in_specs=[pl.BlockSpec(memory_space=pltpu.SMEM)]
        + [pl.BlockSpec(memory_space=pltpu.VMEM)] * 2,
        out_specs=pl.BlockSpec(memory_space=pltpu.VMEM),
        out_shape=jax.ShapeDtypeStruct((rows, total), weight.dtype),
        compiler_params=PARAMS,
        cost_estimate=cost(0, 4 * rows * columns),
        name="pick_heads",
    )(member, weight, other)


def pick_units(weight, member, members, shards):
    rows, columns = weight.shape
    unit = columns // (shards * members)

    def kernel(member_ref, in_ref, out_ref):
        for m in range(members):

            @pl.when(member_ref[0] == m)
            def _():
                out_ref[...] = jnp.concatenate(
                    [
                        in_ref[:, (f * members + m) * unit : (f * members + m + 1) * unit]
                        for f in range(shards)
                    ],
                    axis=1,
                )

    return pl.pallas_call(
        kernel,
        in_specs=[pl.BlockSpec(memory_space=pltpu.SMEM), pl.BlockSpec(memory_space=pltpu.VMEM)],
        out_specs=pl.BlockSpec(memory_space=pltpu.VMEM),
        out_shape=jax.ShapeDtypeStruct((rows, columns // members), weight.dtype),
        compiler_params=PARAMS,
        cost_estimate=cost(0, 2 * rows * columns * 2),
        name="pick_units",
    )(member, weight)


def join_units(parts, shards):
    rows, columns = parts[0].shape
    unit = columns // shards

    def kernel(*refs):
        refs[-1][...] = jnp.concatenate(
            [ref[:, f * unit : (f + 1) * unit] for f in range(shards) for ref in refs[:-1]], axis=1
        )

    return pl.pallas_call(
        kernel,
        in_specs=[pl.BlockSpec(memory_space=pltpu.VMEM)] * len(parts),
        out_specs=pl.BlockSpec(memory_space=pltpu.VMEM),
        out_shape=jax.ShapeDtypeStruct((rows, columns * len(parts)), parts[0].dtype),
        compiler_params=PARAMS,
        cost_estimate=cost(0, 8 * rows * columns * len(parts)),
        name="join_units",
    )(*parts)


def shift_seq(values, amount):
    members = lax.axis_size("seq")
    return lax.ppermute(values, "seq", [(i, (i + amount) % members) for i in range(members)])


def gather_seq(values):
    return [values] + [shift_seq(values, k) for k in range(1, lax.axis_size("seq"))]


def pick(values, index, axis):
    return lax.dynamic_index_in_dim(values, index, axis, keepdims=False)


class Reduction:
    def __init__(self, halves):
        self.terms, self.away = [halves[0]], halves[1]
        self.bit, self.came = 1, None

    def send(self):
        size = lax.axis_size("fsdp")
        self.came = lax.ppermute(self.away, "fsdp", [(i, i ^ self.bit) for i in range(size)])

    def land(self):
        self.terms.append(self.came)
        self.bit, self.came = self.bit * 2, None
        if self.bit < lax.axis_size("fsdp"):
            mine = (lax.axis_index("fsdp") // self.bit) % 2
            terms = [t.reshape((t.shape[0] // 2, 2) + t.shape[1:]) for t in self.terms]
            self.away = sum(pick(t, 1 - mine, 1).astype(F32) for t in terms).astype(BF16)
            self.terms = [pick(t, mine, 1) for t in terms]

    def result(self):
        return sum(t.astype(F32) for t in self.terms)[0]


def gate(first, *others):
    return lax.optimization_barrier((first, *others))


class Order:
    def __init__(self):
        self.marks, self.closed = [], False

    def __call__(self, *arrays):
        if not arrays:
            return []
        self.closed = True
        return list(gate(*arrays, *self.marks)[: len(arrays)])

    def mark(self, *arrays):
        if self.closed:
            self.marks, self.closed = [], False
        self.marks += arrays


def statistics(values):
    average = jnp.mean(values, axis=-1, keepdims=True)
    centred = values - average
    return (average, lax.rsqrt(jnp.mean(centred * centred, axis=-1, keepdims=True) + 1e-06))


def modulated(values, stats, shift, scale):
    return (((values - stats[0]) * stats[1]) * (1.0 + scale) + shift).astype(BF16)


def norm_back(grad, unit, root):
    return root * (
        grad
        - jnp.mean(grad, axis=-1, keepdims=True)
        - unit * jnp.mean(grad * unit, axis=-1, keepdims=True)
    )


def times(left, right):
    return lax.dot_general(left, right, (((2,), (0,)), ((), ())), preferred_element_type=F32)


def times_t(left, right):
    return lax.dot_general(left, right, (((2,), (1,)), ((), ())), preferred_element_type=F32)


def pad_rows(values, rows):
    return jnp.pad(values, ((0, 0), (0, rows - values.shape[1]), (0, 0)))


def body(
    img_in, txt_in, cond, text_counts, ada_w, qkv_w, proj_w, fc1_w, fc2_w, qk_gain, img_cot, txt_cot
):
    members = lax.axis_size("seq")
    member = lax.axis_index("seq")
    shards = lax.axis_size("fsdp")
    sequences, img_local, width = img_in.shape
    slots = txt_in.shape[1]
    padded = -(-slots // 16) * 16
    img_total = members * img_local
    head_width = width // members
    head_padded = -(-head_width // LANES) * LANES
    groups = 2 if (head_padded // LANES) % 2 == 0 else 1
    group_width = head_padded // groups
    hidden_width = fc1_w.shape[2]
    shard_rows = ada_w.shape[1]
    unit_rows = hidden_width // (shards * members)
    member_index = member.reshape(1)
    own_bit = (lax.axis_index("fsdp") % 2).reshape(1)
    every = range(members)
    both = range(sequences)

    txt_in, txt_cot = pad_rows(txt_in, padded), pad_rows(txt_cot, padded)
    img_all, txt_all = gather_seq(img_in), gather_seq(txt_in)
    ready = gate(img_cot, txt_cot, *img_all[1:])
    img_cots, txt_cots = gather_seq(ready[0]), gather_seq(ready[1])

    own_both = pick_heads(
        qkv_w.reshape(2 * shard_rows, 3 * width),
        proj_w.reshape(2 * shard_rows, width),
        member_index,
        members,
        groups,
        group_width,
    )
    w_both = lax.all_gather(own_both.reshape(2, shard_rows, -1), "fsdp", axis=1, tiled=True)
    triple = 3 * head_padded
    w_qkv = [w_both[t, :, :triple] for t in range(2)]
    w_proj = [w_both[t, :, triple:] for t in range(2)]

    cond_act = jax.nn.silu(cond.astype(F32)).astype(BF16)
    cond_cols = lax.all_to_all(
        cond_act.reshape(sequences, shards, shard_rows), "fsdp", split_axis=1, concat_axis=0, tiled=True
    ).reshape(shards * sequences, shard_rows)
    mod_width = ada_w.shape[2]
    share = mod_width // members
    own_ada = lax.dynamic_slice_in_dim(ada_w, member * share, share, 2)
    mod_part = jnp.einsum("sd,tdm->stm", cond_cols, own_ada, preferred_element_type=F32)
    mod_part = mod_part.reshape(shards, sequences, 2, share)
    mod_part, fc1_w, fc2_w = gate(mod_part, fc1_w, fc2_w)
    mod_sum = jnp.sum(
        lax.all_to_all(mod_part, "fsdp", split_axis=0, concat_axis=0, tiled=True), axis=0
    )
    mod_shares = jnp.stack(gather_seq(mod_sum))
    modulation = jnp.concatenate(
        [pick(mod_shares, (member - i) % members, 0) for i in every], axis=-1
    )

    own_fc1 = pick_units(fc1_w.reshape(2 * shard_rows, hidden_width), member_index, members, shards)
    own_fc2 = pick(fc2_w.reshape(2, members, unit_rows, width), member, 1)
    w_fc1 = lax.all_gather(own_fc1.reshape(2, shard_rows, -1), "fsdp", axis=1, tiled=True)
    w_fc2 = lax.all_gather(own_fc2, "fsdp", axis=1, tiled=True)

    counts = jnp.stack([pick(text_counts, (member - k) % members, 1) for k in every], axis=1)
    slot_ids = lax.broadcasted_iota(jnp.int32, (sequences, members, padded), 2)
    live = (slot_ids < counts[:, :, None]).astype(F32)
    live_rows = jnp.transpose(live, (1, 0, 2)).reshape(members * sequences, padded, 1)
    text_rows = live_rows[:sequences]
    live_lanes = jnp.broadcast_to(
        live.reshape(sequences, members * padded, 1), (sequences, members * padded, LANES)
    )
    gains = jnp.tile(qk_gain.reshape(4, HEAD), (1, 2))
    pieces = [
        [piece[:, None, :] for piece in jnp.split(modulation[:, t], 6, axis=-1)] for t in range(2)
    ]

    def text_all(vector):
        return jnp.tile(vector, (members, 1, 1))

    ready = gate(modulation, *img_all[1:], *txt_all[1:])
    img_all, txt_all = [img_all[0], *ready[1:members]], [txt_all[0], *ready[members:]]
    img_f32 = [values.astype(F32) for values in img_all]
    img_stats = [statistics(values) for values in img_f32]
    txt_f32 = jnp.concatenate(txt_all, axis=0).astype(F32)
    txt_stats = statistics(txt_f32)
    normed_img = [modulated(img_f32[k], img_stats[k], pieces[0][0], pieces[0][1]) for k in every]
    normed_txt = modulated(txt_f32, txt_stats, text_all(pieces[1][0]), text_all(pieces[1][1]))
    raw_img = [times(normed_img[k], w_qkv[0]) for k in every]
    raw_txt = times(normed_txt, w_qkv[1])
    raw = [
        [(raw_img[k], s) for k in every] + [(raw_txt, k * sequences + s) for k in every]
        for s in both
    ]
    attended, norms = [], []
    order = Order()
    for s in both:
        values, norm = attend(raw[s], order(gains)[0], live_lanes, s, img_total, groups)
        attended.append(values)
        norms.append(norm)
        order.mark(norm)

    def advance(land, send):
        for red in land:
            if red.came is not None:
                red.came = order(red.came)[0]
                red.land()
                order.mark(*(red.terms if red.bit == shards else [red.away]))
        for red in send:
            if red.bit < shards:
                order.mark(red.away)
                red.send()

    def to_members(parts):
        return [parts[0]] + [shift_seq(parts[k], -k) for k in range(1, members)]

    came_attended = [to_members(attended[s][:members]) for s in both]
    came_attended_txt = [to_members(attended[s][members:]) for s in both]

    came_attended[0] = order(*came_attended[0])
    ready = gate(came_attended[0][0], *order(*img_cots[1:], *txt_cots[1:]))[1:]
    img_cots, txt_cots = [img_cots[0], *ready[: members - 1]], [txt_cots[0], *ready[members - 1 :]]
    mlp_img = [(pieces[0][5] * values.astype(F32)).astype(BF16) for values in img_cots]
    txt_grads = jnp.concatenate(txt_cots, axis=0).astype(F32) * live_rows
    mlp_txt = (text_all(pieces[1][5]) * txt_grads).astype(BF16)
    order.mark(*mlp_img, mlp_txt)

    vectors = [[p[s : s + 1] for p in pieces[0]] for s in both] + [pieces[1]]
    kinds = [0] * sequences + [1]
    units = range(sequences + 1)
    text = sequences

    def own_in():
        img, txt = order(img_in, txt_in)
        return [img[s : s + 1].astype(F32) for s in both] + [txt.astype(F32)]

    def own_grad():
        img, txt = order(img_cot, txt_cot)
        return [img[s : s + 1].astype(F32) for s in both] + [txt.astype(F32) * text_rows]

    def heads_together(parts):
        parts = [part[..., :head_width] for part in parts]
        return jnp.roll(jnp.concatenate(parts, axis=-1), member * head_width, axis=-1)

    own_attended, middle, branch, mid_stats, normed_mid = [], [], [], [], []
    tokens = own_in()
    for u in units:
        t = kinds[u]
        if t == 0:
            own_attended.append(heads_together(order(*came_attended[u])))
        else:
            parts = order(*[part for parts in came_attended_txt for part in parts])
            parts = [parts[s * members : (s + 1) * members] for s in both]
            own_attended.append(
                jnp.concatenate([heads_together(parts[s]) for s in both], axis=0)
            )
        branch.append(times(own_attended[u], w_proj[t]))
        middle.append(tokens[u] + vectors[u][2] * branch[u])
        mid_stats.append(statistics(middle[u]))
        normed = modulated(middle[u], mid_stats[u], vectors[u][3], vectors[u][4])
        order.mark(normed)
        normed_mid.append(gather_seq(normed))

    hidden = [[None] * members for _ in both] + [None]
    mlp_pieces = [[(mlp_img[k], s) for k in every] for s in both]
    mlp_pieces.append([(mlp_txt.reshape(1, -1, width), 0)])

    def rise(u, k):
        values = order(normed_mid[u][k])[0]
        normed_mid[u][k] = values
        hidden[u][k] = times(values, w_fc1[0])
        order.mark(hidden[u][k])

    def reduction(lefts, rights):
        red = Reduction(weight_sum(lefts, rights, shards, own_bit))
        order.mark(red.away)
        return red

    def scattered(lefts, rights):
        summed = weight_sum(lefts, rights, shards)
        order.mark(summed)
        return lax.psum_scatter(summed, "fsdp", scatter_dimension=0, tiled=True)[0, 0]

    def at_first(arrays):
        return [(array, 0) for array in arrays]

    def of(lists, t):
        return [array for u in units if kinds[u] == t for array in lists[u]]

    def to_owners(products):
        return [shift_seq(p.astype(BF16), -k) for k, p in enumerate(products, 1)]

    def text_members(products):
        return jnp.split(products.reshape(-1, padded, width), members, axis=0)

    active, hidden_grad = [None] * len(units), [None] * len(units)
    came_mid = [None] * len(units)
    own_text = {}

    def feed(u):
        t = kinds[u]
        hidden[u][0] = order(hidden[u][0])[0]
        active[u], hidden_grad[u] = hidden_back(
            [(h, 0) for h in hidden[u]], mlp_pieces[u], w_fc2, t
        )
        if t == 0:
            products = [times_t(values, w_fc1[t]).astype(BF16) for values in hidden_grad[u][1:]]
            order.mark(*products)
        else:
            parts = text_members(times_t(hidden_grad[u][0], w_fc1[t]))
            own_text["mid"], products = parts[0], parts[1:]
            order.mark(parts[0])
        came_mid[u] = to_owners(products)

    for s in both:
        rise(s, 0)
    for k in range(1, members):
        rise(0, k)
    values = order(*normed_mid[text])
    normed_mid[text] = [jnp.concatenate(values, axis=0).reshape(1, -1, width)]
    hidden[text] = [times(normed_mid[text][0], w_fc1[1])]
    order.mark(hidden[text][0])
    for s in range(1, sequences):
        for k in range(1, members):
            rise(s, k)
    feed(text)
    ready = order(active[text][0], hidden_grad[text][0])
    fc2_txt = scattered(at_first(ready[:1]), mlp_pieces[text])
    fc1_txt = scattered(at_first(normed_mid[text]), at_first(ready[1:]))
    feed(0)
    for s in range(1, sequences):
        feed(s)
    active[0][0] = order(active[0][0])[0]
    fc2_img = scattered(
        at_first(of(active, 0)), [p for u in units if kinds[u] == 0 for p in mlp_pieces[u]]
    )

    middle_grad, late_grads, head_grads, branch_grad = {}, {}, {}, {}
    grads_now = own_grad()
    for u in [0, text, *range(1, sequences)]:
        t = kinds[u]
        came = order(*came_mid[u])
        if t == 0:
            mid_grad = times_t(hidden_grad[u][0], w_fc1[t])
        else:
            mid_grad = own_text["mid"]
        for values in came:
            mid_grad = mid_grad + values.astype(F32)
        average, root = mid_stats[u]
        unit = (middle[u] - average) * root
        scale_mlp_grad = jnp.sum(mid_grad * unit, axis=1)
        shift_mlp_grad = jnp.sum(mid_grad, axis=1)
        total = grads_now[u] + norm_back(mid_grad * (1.0 + vectors[u][4]), unit, root)
        middle_grad[u] = total
        gate_attn_grad = jnp.sum(total * branch[u], axis=1)
        late_grads[u] = [gate_attn_grad, shift_mlp_grad, scale_mlp_grad]
        branch_grad[u] = (vectors[u][2] * total).astype(BF16)
        attended_grad = times_t(branch_grad[u], w_proj[t]).astype(BF16)
        attended_grad = jnp.roll(attended_grad, -member * head_width, axis=-1)
        parts = []
        for k in every:
            part = attended_grad[..., k * head_width : (k + 1) * head_width]
            if head_padded > head_width:
                part = jnp.pad(part, ((0, 0), (0, 0), (0, head_padded - head_width)))
            parts.append(part)
        order.mark(*parts)
        head_grads[u] = [shift_seq(part, k) if k else part for k, part in enumerate(parts)]
    ready = order(branch_grad[text], branch_grad[0])
    branch_grad[text], branch_grad[0] = ready
    proj_both = None
    for t in range(2):
        proj_both = weight_sum(
            at_first([own_attended[u].reshape(1, -1, width) for u in units if kinds[u] == t]),
            at_first([branch_grad[u].reshape(1, -1, width) for u in units if kinds[u] == t]),
            shards,
            before=proj_both,
            place=t,
            places=2,
        )
    order.mark(proj_both)
    proj_both = lax.psum_scatter(proj_both, "fsdp", scatter_dimension=0, tiled=True)[0]
    hidden_grad[0][0] = order(hidden_grad[0][0])[0]
    fc1_img = reduction(at_first(of(normed_mid, 0)), at_first(of(hidden_grad, 0)))
    advance([], [fc1_img])
    grads = [
        [head_grads[s][k] for k in every] + [head_grads[text][k][s : s + 1] for k in every]
        for s in both
    ]
    steps = {
        (0, 0): [fc1_img],
        (0, groups - 1): [fc1_img],
        (sequences - 1, 0): [fc1_img],
        (sequences - 1, groups - 1): [fc1_img],
    }
    gain_parts, raw_grads, came_in, came_mlp = [], [], [], None

    def in_products(s):
        values = order(*raw_grads[s][1:members])
        products = [times_t(v, w_qkv[0]).astype(BF16) for v in values]
        order.mark(*products)
        return to_owners(products)

    for s in both:
        before = None
        for group in range(groups):
            before, gain_part = attend_back(
                raw[s],
                grads[s],
                attended[s],
                norms[s],
                order(gains)[0],
                live_lanes,
                s,
                img_total,
                groups,
                group,
                before,
            )
            gain_parts.append(gain_part)
            order.mark(gain_part)
            reds = steps.pop((s, group), [])
            advance(reds, reds)
        raw_grads.append(before)
        if came_mlp is None:
            came_mlp = []
            for u in units:
                values = order(*active[u])
                active[u] = values
                if kinds[u] == 0:
                    products = [times(v, w_fc2[0]).astype(BF16) for v in values[1:]]
                    order.mark(*products)
                else:
                    parts = text_members(times(values[0], w_fc2[1]))
                    own_text["mlp"], products = parts[0], parts[1:]
                    order.mark(parts[0])
                came_mlp.append(to_owners(products))
        if s < sequences - 1:
            came_in.append(in_products(s))
    came_mlp = [order(*came) for came in came_mlp]
    values = gate(*order(*raw_grads[-1][:members]), *[v for came in came_mlp for v in came])[:members]
    raw_grads[-1] = [*values, *raw_grads[-1][members:]]
    qkv_img = reduction(
        [(normed_img[k], s) for s in both for k in every],
        at_first([raw_grads[s][k] for s in both for k in every]),
    )
    advance([], [qkv_img])
    came_in.append(in_products(sequences - 1))
    advance([qkv_img], [qkv_img])
    raw_text = jnp.concatenate([raw_grads[s][members + k] for k in every for s in both], axis=0)
    raw_text = order(raw_text)[0]
    parts = text_members(times_t(raw_text, w_qkv[1]))
    own_text["in"] = parts[0]
    came_in.append(to_owners(parts[1:]))
    order.mark(parts[0])
    raw_text = order(raw_text)[0]
    qkv_txt = reduction(
        at_first([normed_txt.reshape(1, -1, width)]), at_first([raw_text.reshape(1, -1, triple)])
    )
    advance([], [qkv_txt])
    in_grads, in_sums, outs, gate_sums = {}, {}, {}, {}
    tokens = own_in()

    def input_back(u):
        came = order(*came_in[u])
        in_grad = times_t(raw_grads[u][0], w_qkv[0]) if kinds[u] == 0 else own_text["in"]
        for values in came:
            in_grad = in_grad + values.astype(F32)
        average, root = statistics(tokens[u])
        unit = (tokens[u] - average) * root
        in_sums[u] = [jnp.sum(in_grad, axis=1), jnp.sum(in_grad * unit, axis=1)]
        in_grads[u] = middle_grad[u] + norm_back(in_grad * (1.0 + vectors[u][1]), unit, root)
        order.mark(in_grads[u], *in_sums[u])

    def output(u):
        came = order(*came_mlp[u])
        mlp_out = times(active[u][0], w_fc2[0]) if kinds[u] == 0 else own_text["mlp"]
        for values in came:
            mlp_out = mlp_out + values.astype(F32)
        result = middle[u] + vectors[u][5] * mlp_out
        if kinds[u] == 1:
            result = result * text_rows
        outs[u] = result.astype(BF16)
        gate_sums[u] = jnp.sum(grads_late[u] * mlp_out, axis=1)
        order.mark(outs[u], gate_sums[u])

    advance([qkv_txt], [qkv_txt])
    grads_late = own_grad()
    for s in range(sequences - 1):
        input_back(s)
    output(0)
    advance([qkv_img], [qkv_img])
    input_back(text)
    input_back(sequences - 1)
    for u in units:
        if u:
            output(u)
    mod_rows = [
        jnp.concatenate([*in_sums[u], *late_grads[u], gate_sums[u]], axis=-1) for u in units
    ]
    img_out = jnp.concatenate([outs[s] for s in both], axis=0)
    txt_out = outs[text][:, :slots]
    img_grad = jnp.concatenate([in_grads[s] for s in both], axis=0)
    txt_grad = in_grads[text][:, :slots]

    gain_own = sum(jnp.sum(part, axis=0) for part in gain_parts)[:4]
    gain_own = (gain_own[:, :HEAD] + gain_own[:, HEAD:]).reshape(-1)
    mod_own = jnp.stack([jnp.concatenate(mod_rows[:-1], axis=0), mod_rows[-1]], axis=1)
    mod_count = mod_own.size
    own_shared = jnp.concatenate([mod_own.reshape(-1), gain_own])
    order.mark(own_shared)
    came_shared = gather_seq(own_shared)[1:]
    qkv_red = [qkv_img, qkv_txt]
    advance(qkv_red, qkv_red)
    shared = sum(order(*came_shared), own_shared)
    gain_high = shared[mod_count:].astype(BF16)
    gain_low = (shared[mod_count:] - gain_high.astype(F32)).astype(BF16)
    packed = jnp.concatenate([shared[:mod_count].astype(BF16), gain_high, gain_low])[None]
    order.mark(packed)
    packed = lax.all_gather(packed, "fsdp", axis=0, tiled=True)

    def finish(reds):
        while reds:
            advance(reds, reds)
            reds = [red for red in reds if red.bit < shards]

    def send_rows(values):
        blocks = values.reshape((members, -1) + values.shape[1:])
        own = pick(blocks, member, 0)
        parts = [pick(blocks, (member + k) % members, 0) for k in range(1, members)]
        order.mark(own, *parts)
        return [own] + [shift_seq(part, k) for k, part in enumerate(parts, 1)]

    def by_place(parts):
        stacked = jnp.stack([parts[0], *order(*parts[1:])])
        return [pick(stacked, (member - i) % members, 0) for i in every]

    finish([fc1_img])
    ready = order(fc2_img, fc2_txt, fc1_txt, proj_both)
    fc2_grad = jnp.stack(ready[:2]).astype(F32)
    fc1_rows = [send_rows(fc1_img.result()), send_rows(ready[2].astype(F32))]
    proj_rows = send_rows(jnp.transpose(ready[3].astype(F32), (1, 0, 2)))
    advance(qkv_red, qkv_red)
    fc1_grad = jnp.stack([join_units(by_place(rows), shards) for rows in fc1_rows])
    proj_grad = jnp.transpose(sum(order(*proj_rows[1:]), proj_rows[0]), (1, 0, 2))
    order.mark(fc1_grad, proj_grad)
    advance(qkv_red, qkv_red)

    packed = order(packed)[0]
    every_mod = packed[:, :mod_count].reshape(shards * sequences, 2, mod_width)
    gain_grad = jnp.sum(packed[:, mod_count:].astype(F32), axis=0).reshape(2, 2, 2 * HEAD).sum(axis=0)
    cond_part = jnp.einsum("stm,tdm->sd", every_mod, ada_w, preferred_element_type=F32)
    order.mark(cond_part)
    cond_full = lax.all_to_all(cond_part, "fsdp", split_axis=0, concat_axis=1, tiled=True)
    finish(qkv_red)
    qkv_rows = [send_rows(red.result()) for red in qkv_red]
    every_mod = order(every_mod)[0]
    out_rows = width // (shards * members)
    own_cols = lax.dynamic_slice_in_dim(cond_cols, member * out_rows, out_rows, 1)
    ada_grad = jnp.einsum("sr,stm->trm", own_cols, every_mod, preferred_element_type=F32)
    cond_grad = jax.vjp(jax.nn.silu, cond.astype(F32))[1](cond_full)[0]
    qkv_grad = []
    for rows in qkv_rows:
        parts = by_place(rows)
        qkv_grad.append(
            jnp.concatenate(
                [
                    parts[m][:, (g * 3 + part) * group_width :][
                        :, : min(group_width, head_width - g * group_width)
                    ]
                    for part in range(3)
                    for m in every
                    for g in range(groups)
                ],
                axis=1,
            )
        )
    qkv_grad = jnp.stack(qkv_grad)
    return (
        img_out,
        txt_out,
        img_grad,
        txt_grad,
        cond_grad,
        ada_grad,
        qkv_grad,
        proj_grad,
        fc1_grad,
        fc2_grad,
        gain_grad,
    )


def solution(mesh):
    tokens, rows = P("fsdp", "seq", None), P("fsdp", None)
    weight, weight_grad = P(None, "fsdp", None), P(None, ("fsdp", "seq"), None)
    in_specs = (tokens, tokens, rows, rows) + (weight,) * 5 + (P(), tokens, tokens)
    out_specs = (tokens,) * 4 + (rows,) + (weight_grad,) * 5 + (P(),)
    return jax.shard_map(body, mesh=mesh, in_specs=in_specs, out_specs=out_specs, check_vma=False)
```

```python
import math

import jax
import jax.numpy as jnp
from jax import lax
from jax.experimental import pallas as pl
from jax.experimental.pallas import tpu as pltpu
from jax.sharding import PartitionSpec as P

HEAD = 64
LANES = 128
BLOCK = 512
BF16 = jnp.bfloat16
F32 = jnp.float32
SCALE = HEAD**-0.5
SCALE2 = SCALE * math.log2(math.e)
VMEM_LIMIT = 56 * 1024 * 1024
NT = (((1,), (1,)), ((), ()))
NN = (((1,), (0,)), ((), ()))


def dot(left, right, dims=NN):
    return lax.dot_general(left, right, dims, preferred_element_type=F32)


def low_lanes():
    return lax.broadcasted_iota(jnp.int32, (1, LANES), 1) < HEAD


def head_mean(values):
    low = low_lanes()
    first = jnp.sum(jnp.where(low, values, 0.0), axis=-1, keepdims=True)
    second = jnp.sum(jnp.where(low, 0.0, values), axis=-1, keepdims=True)
    return jnp.where(low, first, second) * (1.0 / HEAD)


def rms(values):
    return lax.rsqrt(head_mean(values * values) + 1e-06)


def blocks_of(total, size):
    return [(start, min(size, total - start)) for start in range(0, total, size)]


def attend_kernel(rows, img_total, *refs):
    count = len(rows)
    raw, refs = refs[: 3 * count], refs[3 * count :]
    gain_ref, live_ref = refs[:2]
    out, refs = refs[2 : 2 + count], refs[2 + count :]
    norm_ref, q_s, k0_s, k1_s, v0_s, v1_s, o_s = refs
    low = low_lanes()
    offset = 0
    for i, size in enumerate(rows):
        text = offset >= img_total
        place = pl.ds(offset, size)
        gain = 2 if text else 0
        query, key, value = (raw[3 * i + part][0] for part in range(3))
        q_s[place, :] = (query * rms(query) * gain_ref[gain : gain + 1, :]).astype(BF16)
        key = key * rms(key) * gain_ref[gain + 1 : gain + 2, :]
        k0_s[place, :] = jnp.where(low, key, 0.0).astype(BF16)
        k1_s[place, :] = jnp.where(low, 0.0, key).astype(BF16)
        if text:
            live = live_ref[0, pl.ds(offset - img_total, size), :]
            value = value * live
        else:
            live = jnp.ones_like(value)
        v0_s[place, :] = jnp.where(low, value, live).astype(BF16)
        v1_s[place, :] = jnp.where(low, live, value).astype(BF16)
        offset += size

    def block(start, size):
        place = pl.ds(start, size)
        query = q_s[place, :]
        sums = []
        for key_ref, value_ref in ((k0_s, v0_s), (k1_s, v1_s)):
            weights = jnp.exp2(dot(query, key_ref[...], NT) * SCALE2).astype(BF16)
            sums.append(dot(weights, value_ref[...]))
        top = jnp.where(low, sums[0], sums[1])
        bottom = pltpu.roll(jnp.where(low, sums[1], sums[0]), HEAD, 1)
        o_s[place, :] = (top / bottom).astype(BF16)
        turned = jnp.log2(bottom).T
        norm_ref[0, 0, 0:8, place] = turned[0:8]
        norm_ref[0, 0, 8:16, place] = turned[HEAD : HEAD + 8]

    def step(i, carry):
        block(pl.multiple_of(i * BLOCK, BLOCK), BLOCK)
        return carry

    lax.fori_loop(0, img_total // BLOCK, step, 0)
    for start, size in blocks_of(offset - img_total, BLOCK):
        block(img_total + start, size)
    offset = 0
    for i, size in enumerate(rows):
        out[i][0] = o_s[pl.ds(offset, size), :]
        offset += size


def attend_back_kernel(rows, img_total, width, *refs):
    count = len(rows)
    raw, refs = refs[: 3 * count], refs[3 * count :]
    grad, refs = refs[:count], refs[count:]
    done, refs = refs[:count], refs[count:]
    norm_ref, gain_ref, live_ref = refs[:3]
    out, refs = refs[3 : 3 + count], refs[3 + count :]
    gain_out, q_s, k_s, v_s, kt_s, do_s, o_s, dq_s, dk_s, dv_s = refs
    low = low_lanes()
    pair = pl.program_id(0)
    offset = 0
    for i, size in enumerate(rows):
        text = offset >= img_total
        place = pl.ds(offset, size)
        gain = 2 if text else 0
        query, key, value = (raw[3 * i + part][0] for part in range(3))
        q_s[place, :] = (query * rms(query) * gain_ref[gain : gain + 1, :]).astype(BF16)
        key = (key * rms(key) * gain_ref[gain + 1 : gain + 2, :]).astype(BF16)
        k_s[place, :] = key
        v_s[place, :] = value.astype(BF16)
        do_s[place, :] = grad[i][0]
        o_s[place, :] = done[i][0]
        offset += size
    total = offset
    key_blocks = blocks_of(img_total, BLOCK) + [
        (img_total + start, size) for start, size in blocks_of(total - img_total, BLOCK)
    ]
    for start, size in key_blocks:
        key = k_s[pl.ds(start, size), :].astype(F32)
        if start >= img_total:
            key = key * live_ref[0, pl.ds(start - img_total, size), :]
        kt_s[:, pl.ds(start, size)] = key.T.astype(BF16)
    dk_s[...] = jnp.zeros_like(dk_s)
    dv_s[...] = jnp.zeros_like(dv_s)

    def block(start, size):
        place = pl.ds(start, size)
        query = q_s[place, :]
        grads = do_s[place, :]
        both = (grads.astype(F32) * o_s[place, :].astype(F32)).T
        side = []
        for h in range(2):
            delta = jnp.sum(both[h * HEAD : (h + 1) * HEAD], axis=0, keepdims=True)
            norm = norm_ref[0, 0, 8 * h : 8 * h + 1, place]
            own = low if h == 0 else jnp.logical_not(low)
            query_h = jnp.where(own, query, jnp.zeros_like(query))
            grads_h = jnp.where(own, grads, jnp.zeros_like(grads))
            side.append((delta, norm, query_h, grads_h))
        probs, changes = [], []
        for delta, norm, query_h, grads_h in side:
            prob = jnp.exp2(dot(k_s[...], query_h, NT) * SCALE2 - norm)
            prob_grad = dot(v_s[...], grads_h, NT)
            changes.append((prob * (prob_grad - delta)).astype(BF16))
            probs.append(prob.astype(BF16))
        dv_s[...] += dot(probs[0], side[0][3]) + dot(probs[1], side[1][3])
        dk_s[...] += dot(changes[0], side[0][2]) + dot(changes[1], side[1][2])
        turned = [dot(kt_s[h * HEAD : (h + 1) * HEAD, :], changes[h]) for h in range(2)]
        dq_s[place, :] = jnp.concatenate(turned, axis=0).T

    def step(i, carry):
        block(pl.multiple_of(i * BLOCK, BLOCK), BLOCK)
        return carry

    lax.fori_loop(0, img_total // BLOCK, step, 0)
    for start, size in blocks_of(total - img_total, BLOCK):
        block(img_total + start, size)

    gain_sums = [jnp.zeros((1, LANES), F32) for _ in range(4)]
    offset = 0
    for i, size in enumerate(rows):
        text = offset >= img_total
        place = pl.ds(offset, size)
        value_grad = dv_s[place, :]
        key_grad = dk_s[place, :]
        if text:
            live = live_ref[0, pl.ds(offset - img_total, size), :]
            value_grad = value_grad * live
            key_grad = key_grad * live
        for part, change in enumerate((dq_s[place, :], key_grad)):
            row = (2 if text else 0) + part
            change = (change * SCALE).astype(BF16).astype(F32)
            values = raw[3 * i + part][0]
            root = rms(values)
            unit = values * root
            gain_sums[row] += jnp.sum(change * unit, axis=0, keepdims=True)
            change = change * gain_ref[row : row + 1, :]
            change = root * (change - unit * head_mean(change * unit))
            column = pl.multiple_of(part * width + pair * LANES, LANES)
            out[i][0, :, pl.ds(column, LANES)] = change.astype(BF16)
        column = pl.multiple_of(2 * width + pair * LANES, LANES)
        out[i][0, :, pl.ds(column, LANES)] = value_grad.astype(BF16)
        offset += size
    for row in range(4):
        gain_out[0, row : row + 1, :] = gain_sums[row]
    gain_out[0, 4:8, :] = jnp.zeros((4, LANES), F32)


def cost(flops, bytes_accessed, transcendentals=0):
    return pl.CostEstimate(
        flops=flops, bytes_accessed=bytes_accessed, transcendentals=transcendentals
    )


PARAMS = pltpu.CompilerParams(vmem_limit_bytes=VMEM_LIMIT)


def raw_specs(raw, group, count):
    return [
        pl.BlockSpec(
            (1, array.shape[1], LANES),
            lambda p, sel=sel, part=part: (sel, 0, (group * 3 + part) * count + p),
        )
        for array, sel in raw
        for part in range(3)
    ]


def rows_of(pieces):
    return [array.shape[1] for array, _ in pieces]


def attend(raw, gains, live, sequence, img_total, groups):
    width = raw[0][0].shape[2] // 3
    pairs = width // LANES
    count = pairs // groups
    rows = rows_of(raw)
    total = sum(rows)

    def kernel(*refs):
        attend_kernel(rows, img_total, *refs)

    work = pairs * 2 * total * total
    outputs = pl.pallas_call(
        kernel,
        grid=(pairs,),
        in_specs=[
            pl.BlockSpec(
                (1, array.shape[1], LANES),
                lambda p, sel=sel, part=part: (
                    sel,
                    0,
                    (p // count * 3 + part) * count + p % count,
                ),
            )
            for array, sel in raw
            for part in range(3)
        ]
        + [
            pl.BlockSpec((4, LANES), lambda p: (0, 0)),
            pl.BlockSpec((1, total - img_total, LANES), lambda p: (sequence, 0, 0)),
        ],
        out_specs=[pl.BlockSpec((1, size, LANES), lambda p: (0, 0, p)) for size in rows]
        + [pl.BlockSpec((1, 1, 16, total), lambda p: (0, p, 0, 0))],
        out_shape=[jax.ShapeDtypeStruct((1, size, width), BF16) for size in rows]
        + [jax.ShapeDtypeStruct((1, pairs, 16, total), F32)],
        scratch_shapes=[pltpu.VMEM((total, LANES), BF16)] * 6,
        compiler_params=PARAMS,
        cost_estimate=cost(work * 4 * LANES, total * width * 14, work),
        name="attend",
    )(*[array for array, _ in raw for _ in range(3)], gains, live)
    return (list(outputs[:-1]), outputs[-1])


def attend_back(raw, grads, done, norm, gains, live, sequence, img_total, groups, group, before):
    triple = raw[0][0].shape[2]
    width = triple // 3
    pairs = width // LANES
    count = pairs // groups
    rows = rows_of(raw)
    total = sum(rows)
    pieces = len(rows)

    def kernel(*refs):
        if before is not None:
            refs = refs[pieces:]
        attend_back_kernel(rows, img_total, count * LANES, *refs)

    head_specs = [
        pl.BlockSpec((1, size, LANES), lambda p: (0, 0, group * count + p)) for size in rows
    ]
    in_specs = (
        raw_specs(raw, group, count)
        + head_specs
        + head_specs
        + [
            pl.BlockSpec((1, 1, 16, total), lambda p: (0, group * count + p, 0, 0)),
            pl.BlockSpec((4, LANES), lambda p: (0, 0)),
            pl.BlockSpec((1, total - img_total, LANES), lambda p: (sequence, 0, 0)),
        ]
    )
    operands = [array for array, _ in raw for _ in range(3)]
    operands += [*grads, *done, norm, gains, live]
    aliases = {}
    if before is not None:
        in_specs = [pl.BlockSpec(memory_space=pl.ANY)] * pieces + in_specs
        operands = list(before) + operands
        aliases = {i: i for i in range(pieces)}
    work = count * 2 * total * total
    outputs = pl.pallas_call(
        kernel,
        grid=(count,),
        in_specs=in_specs,
        out_specs=[
            pl.BlockSpec((1, size, 3 * count * LANES), lambda p: (0, 0, group)) for size in rows
        ]
        + [pl.BlockSpec((1, 8, LANES), lambda p: (p, 0, 0))],
        out_shape=[jax.ShapeDtypeStruct((1, size, triple), BF16) for size in rows]
        + [jax.ShapeDtypeStruct((count, 8, LANES), F32)],
        scratch_shapes=[pltpu.VMEM((total, LANES), BF16)] * 3
        + [pltpu.VMEM((LANES, total), BF16)]
        + [pltpu.VMEM((total, LANES), BF16)] * 2
        + [pltpu.VMEM((total, LANES), F32)] * 3,
        compiler_params=PARAMS,
        input_output_aliases=aliases,
        cost_estimate=cost(work * 10 * LANES, total * count * LANES * 22, work),
        name="attend_back",
    )(*operands)
    return (list(outputs[:-1]), outputs[-1])


def tile_of(extent):
    for size in (1024, 768, 512, 384, 256, 128):
        if extent % size == 0:
            return size
    return extent


def feed_forward(values, grads, weight_in, weight_out, modality):
    width = weight_out.shape[2]
    units = weight_out.shape[1]
    tile = tile_of(units)
    rows = rows_of(values)
    count = len(rows)

    def kernel(*refs):
        in_ref, out_ref = refs[2 * count : 2 * count + 2]
        slope = math.sqrt(2 / math.pi)
        for i in range(count):
            value = dot(refs[i][0], in_ref[0])
            grad = dot(refs[count + i][0], out_ref[0], NT)
            square = value * value
            bent = jnp.tanh(value * (slope + (slope * 0.044715) * square))
            half = 0.5 * value
            rise = 0.5 + 0.5 * bent
            refs[2 * count + 2 + i][0] = (value * rise).astype(BF16)
            rise = rise + half * (1.0 - bent * bent) * (slope + (3 * slope * 0.044715) * square)
            refs[3 * count + 2 + i][0] = (grad * rise).astype(BF16)

    total = sum(rows)
    outputs = pl.pallas_call(
        kernel,
        grid=(units // tile,),
        in_specs=[
            pl.BlockSpec((1, size, width), lambda j, sel=sel: (sel, 0, 0))
            for (_, sel), size in zip(list(values) + list(grads), rows * 2)
        ]
        + [
            pl.BlockSpec((1, width, tile), lambda j: (modality, 0, j)),
            pl.BlockSpec((1, tile, width), lambda j: (modality, j, 0)),
        ],
        out_specs=[pl.BlockSpec((1, size, tile), lambda j: (0, 0, j)) for size in rows] * 2,
        out_shape=[jax.ShapeDtypeStruct((1, size, units), BF16) for size in rows] * 2,
        compiler_params=PARAMS,
        cost_estimate=cost(
            4 * total * width * units, total * 4 * (width + units) + 4 * units * width, total * units
        ),
        name="feed_forward",
    )(*[a for a, _ in values], *[a for a, _ in grads], weight_in, weight_out)
    return (list(outputs[:count]), list(outputs[count:]))


def weight_sum(lefts, rights, blocks, bit=None, before=None, place=0, places=1):
    rows = lefts[0][0].shape[2]
    columns = rights[0][0].shape[2]
    block = rows // blocks
    row_tile = max(size for size in (768, 512, 384, rows) if rows % size == 0 and size % (2 * block) == 0)
    tile = tile_of(columns)
    sizes = rows_of(lefts)
    count = len(sizes)
    run = row_tile // block

    def kernel(*refs):
        bit_ref, refs = refs[0], refs[len(first) :]
        total = None
        for i in range(count):
            part = lax.dot_general(
                refs[i][0], refs[count + i][0], (((0,), (0,)), ((), ())), preferred_element_type=F32
            )
            total = part if total is None else total + part
        if bit is None:
            for j in range(run):
                refs[2 * count][j, 0] = total[j * block : (j + 1) * block].astype(BF16)
        else:
            keep_ref, away_ref = refs[2 * count :]
            odd = bit_ref[0] == 1
            for j in range(run // 2):
                even_rows = total[2 * j * block : (2 * j + 1) * block]
                odd_rows = total[(2 * j + 1) * block : (2 * j + 2) * block]
                keep_ref[j, 0] = jnp.where(odd, odd_rows, even_rows).astype(BF16)
                away_ref[j, 0] = jnp.where(odd, even_rows, odd_rows).astype(BF16)

    total = sum(sizes)
    if bit is None:
        arrays, divide = 1, 1
    else:
        arrays, divide = 2, 2
    out_shape = [jax.ShapeDtypeStruct((blocks // divide, places, block, columns), BF16)] * arrays
    out_specs = [
        pl.BlockSpec((run // divide, 1, block, tile), lambda i, j: (i, place, 0, j))
    ] * arrays
    first_specs, first, aliases = [], [], {}
    if bit is not None:
        first_specs, first = [pl.BlockSpec(memory_space=pltpu.SMEM)], [bit]
    if before is not None:
        aliases = {len(first) + i: i for i in range(arrays)}
        first_specs = first_specs + [pl.BlockSpec(memory_space=pl.ANY)] * arrays
        first = first + list(before)
    return pl.pallas_call(
        kernel,
        grid=(rows // row_tile, columns // tile),
        in_specs=first_specs
        + [
            pl.BlockSpec((1, size, row_tile), lambda i, j, sel=sel: (sel, 0, i))
            for (_, sel), size in zip(lefts, sizes)
        ]
        + [
            pl.BlockSpec((1, size, tile), lambda i, j, sel=sel: (sel, 0, j))
            for (_, sel), size in zip(rights, sizes)
        ],
        out_specs=out_specs,
        out_shape=out_shape,
        compiler_params=PARAMS,
        input_output_aliases=aliases,
        cost_estimate=cost(
            2 * total * rows * columns, 2 * (total * (rows + columns) + rows * columns)
        ),
        name="weight_sum",
    )(*first, *[a for a, _ in lefts], *[a for a, _ in rights])


def pick_heads(weight, other, member, members, groups, group_width):
    rows, columns = weight.shape
    width = columns // 3
    head_width = width // members
    size = lambda group: min(group_width, head_width - group * group_width)

    def kernel(member_ref, in_ref, other_ref, out_ref):
        for m in range(members):

            @pl.when(member_ref[0] == m)
            def _():
                for group in range(groups):
                    for part in range(3):
                        start = part * width + m * head_width + group * group_width
                        piece = in_ref[:, start : start + size(group)]
                        if size(group) < group_width:
                            blank = jnp.zeros((rows, group_width - size(group)), piece.dtype)
                            piece = jnp.concatenate([piece, blank], axis=1)
                        place = (group * 3 + part) * group_width
                        out_ref[:, place : place + group_width] = piece

        out_ref[:, 3 * groups * group_width :] = other_ref[...]

    total = 3 * groups * group_width + other.shape[1]
    return pl.pallas_call(
        kernel,
        in_specs=[pl.BlockSpec(memory_space=pltpu.SMEM)]
        + [pl.BlockSpec(memory_space=pltpu.VMEM)] * 2,
        out_specs=pl.BlockSpec(memory_space=pltpu.VMEM),
        out_shape=jax.ShapeDtypeStruct((rows, total), weight.dtype),
        compiler_params=PARAMS,
        cost_estimate=cost(0, 4 * rows * columns),
        name="pick_heads",
    )(member, weight, other)


def pick_units(weight, member, members, shards):
    rows, columns = weight.shape
    unit = columns // (shards * members)

    def kernel(member_ref, in_ref, out_ref):
        for m in range(members):

            @pl.when(member_ref[0] == m)
            def _():
                out_ref[...] = jnp.concatenate(
                    [
                        in_ref[:, (f * members + m) * unit : (f * members + m + 1) * unit]
                        for f in range(shards)
                    ],
                    axis=1,
                )

    return pl.pallas_call(
        kernel,
        in_specs=[pl.BlockSpec(memory_space=pltpu.SMEM), pl.BlockSpec(memory_space=pltpu.VMEM)],
        out_specs=pl.BlockSpec(memory_space=pltpu.VMEM),
        out_shape=jax.ShapeDtypeStruct((rows, columns // members), weight.dtype),
        compiler_params=PARAMS,
        cost_estimate=cost(0, 2 * rows * columns * 2),
        name="pick_units",
    )(member, weight)


def join_units(parts, shards):
    rows, columns = parts[0].shape
    unit = columns // shards

    def kernel(*refs):
        refs[-1][...] = jnp.concatenate(
            [ref[:, f * unit : (f + 1) * unit] for f in range(shards) for ref in refs[:-1]], axis=1
        )

    return pl.pallas_call(
        kernel,
        in_specs=[pl.BlockSpec(memory_space=pltpu.VMEM)] * len(parts),
        out_specs=pl.BlockSpec(memory_space=pltpu.VMEM),
        out_shape=jax.ShapeDtypeStruct((rows, columns * len(parts)), parts[0].dtype),
        compiler_params=PARAMS,
        cost_estimate=cost(0, 8 * rows * columns * len(parts)),
        name="join_units",
    )(*parts)


def shift_seq(values, amount):
    members = lax.axis_size("seq")
    return lax.ppermute(values, "seq", [(i, (i + amount) % members) for i in range(members)])


def gather_seq(values):
    return [values] + [shift_seq(values, k) for k in range(1, lax.axis_size("seq"))]


def pick(values, index, axis):
    return lax.dynamic_index_in_dim(values, index, axis, keepdims=False)


class Reduction:
    def __init__(self, halves):
        self.terms, self.away = [halves[0]], halves[1]
        self.bit, self.came = 1, None

    def send(self):
        size = lax.axis_size("fsdp")
        self.came = lax.ppermute(self.away, "fsdp", [(i, i ^ self.bit) for i in range(size)])

    def land(self):
        self.terms.append(self.came)
        self.bit, self.came = self.bit * 2, None
        if self.bit < lax.axis_size("fsdp"):
            mine = (lax.axis_index("fsdp") // self.bit) % 2
            terms = [t.reshape((t.shape[0] // 2, 2) + t.shape[1:]) for t in self.terms]
            self.away = sum(pick(t, 1 - mine, 1).astype(F32) for t in terms).astype(BF16)
            self.terms = [pick(t, mine, 1) for t in terms]

    def result(self):
        return sum(t.astype(F32) for t in self.terms)[0]


def gate(first, *others):
    return lax.optimization_barrier((first, *others))


class Order:
    def __init__(self):
        self.marks, self.closed = [], False

    def __call__(self, *arrays):
        if not arrays:
            return []
        self.closed = True
        return list(gate(*arrays, *self.marks)[: len(arrays)])

    def mark(self, *arrays):
        if self.closed:
            self.marks, self.closed = [], False
        self.marks += arrays


def statistics(values):
    average = jnp.mean(values, axis=-1, keepdims=True)
    centred = values - average
    return (average, lax.rsqrt(jnp.mean(centred * centred, axis=-1, keepdims=True) + 1e-06))


def modulated(values, stats, shift, scale):
    return (((values - stats[0]) * stats[1]) * (1.0 + scale) + shift).astype(BF16)


def norm_back(grad, unit, root):
    return root * (
        grad
        - jnp.mean(grad, axis=-1, keepdims=True)
        - unit * jnp.mean(grad * unit, axis=-1, keepdims=True)
    )


def times(left, right):
    return lax.dot_general(left, right, (((2,), (0,)), ((), ())), preferred_element_type=F32)


def times_t(left, right):
    return lax.dot_general(left, right, (((2,), (1,)), ((), ())), preferred_element_type=F32)


def pad_rows(values, rows):
    return jnp.pad(values, ((0, 0), (0, rows - values.shape[1]), (0, 0)))


def body(
    img_in, txt_in, cond, text_counts, ada_w, qkv_w, proj_w, fc1_w, fc2_w, qk_gain, img_cot, txt_cot
):
    members = lax.axis_size("seq")
    member = lax.axis_index("seq")
    shards = lax.axis_size("fsdp")
    sequences, img_local, width = img_in.shape
    slots = txt_in.shape[1]
    padded = -(-slots // 16) * 16
    img_total = members * img_local
    head_width = width // members
    head_padded = -(-head_width // LANES) * LANES
    groups = 2 if (head_padded // LANES) % 2 == 0 else 1
    group_width = head_padded // groups
    hidden_width = fc1_w.shape[2]
    shard_rows = ada_w.shape[1]
    unit_rows = hidden_width // (shards * members)
    member_index = member.reshape(1)
    own_bit = (lax.axis_index("fsdp") % 2).reshape(1)
    every = range(members)
    both = range(sequences)

    txt_in, txt_cot = pad_rows(txt_in, padded), pad_rows(txt_cot, padded)
    img_all, txt_all = gather_seq(img_in), gather_seq(txt_in)
    ready = gate(img_cot, txt_cot, *img_all[1:])
    img_cots, txt_cots = gather_seq(ready[0]), gather_seq(ready[1])

    own_both = pick_heads(
        qkv_w.reshape(2 * shard_rows, 3 * width),
        proj_w.reshape(2 * shard_rows, width),
        member_index,
        members,
        groups,
        group_width,
    )
    w_both = lax.all_gather(own_both.reshape(2, shard_rows, -1), "fsdp", axis=1, tiled=True)
    triple = 3 * head_padded
    w_qkv = [w_both[t, :, :triple] for t in range(2)]
    w_proj = [w_both[t, :, triple:] for t in range(2)]

    cond_act = jax.nn.silu(cond.astype(F32)).astype(BF16)
    cond_cols = lax.all_to_all(
        cond_act.reshape(sequences, shards, shard_rows), "fsdp", split_axis=1, concat_axis=0, tiled=True
    ).reshape(shards * sequences, shard_rows)
    mod_width = ada_w.shape[2]
    share = mod_width // members
    own_ada = lax.dynamic_slice_in_dim(ada_w, member * share, share, 2)
    mod_part = jnp.einsum("sd,tdm->stm", cond_cols, own_ada, preferred_element_type=F32)
    mod_part = mod_part.reshape(shards, sequences, 2, share)
    mod_part, fc1_w, fc2_w = gate(mod_part, fc1_w, fc2_w)
    mod_sum = jnp.sum(
        lax.all_to_all(mod_part, "fsdp", split_axis=0, concat_axis=0, tiled=True), axis=0
    )
    mod_shares = jnp.stack(gather_seq(mod_sum))
    modulation = jnp.concatenate(
        [pick(mod_shares, (member - i) % members, 0) for i in every], axis=-1
    )

    own_fc1 = pick_units(fc1_w.reshape(2 * shard_rows, hidden_width), member_index, members, shards)
    own_fc2 = pick(fc2_w.reshape(2, members, unit_rows, width), member, 1)
    w_fc1 = lax.all_gather(own_fc1.reshape(2, shard_rows, -1), "fsdp", axis=1, tiled=True)
    w_fc2 = lax.all_gather(own_fc2, "fsdp", axis=1, tiled=True)

    counts = jnp.stack([pick(text_counts, (member - k) % members, 1) for k in every], axis=1)
    slot_ids = lax.broadcasted_iota(jnp.int32, (sequences, members, padded), 2)
    live = (slot_ids < counts[:, :, None]).astype(F32)
    live_rows = jnp.transpose(live, (1, 0, 2)).reshape(members * sequences, padded, 1)
    text_rows = live_rows[:sequences]
    live_lanes = jnp.broadcast_to(
        live.reshape(sequences, members * padded, 1), (sequences, members * padded, LANES)
    )
    gains = jnp.tile(qk_gain.reshape(4, HEAD), (1, 2))
    pieces = [
        [piece[:, None, :] for piece in jnp.split(modulation[:, t], 6, axis=-1)] for t in range(2)
    ]

    def text_all(vector):
        return jnp.tile(vector, (members, 1, 1))

    ready = gate(modulation, *img_all[1:], *txt_all[1:])
    img_all, txt_all = [img_all[0], *ready[1:members]], [txt_all[0], *ready[members:]]
    img_f32 = [values.astype(F32) for values in img_all]
    img_stats = [statistics(values) for values in img_f32]
    txt_f32 = jnp.concatenate(txt_all, axis=0).astype(F32)
    txt_stats = statistics(txt_f32)
    normed_img = [modulated(img_f32[k], img_stats[k], pieces[0][0], pieces[0][1]) for k in every]
    normed_txt = modulated(txt_f32, txt_stats, text_all(pieces[1][0]), text_all(pieces[1][1]))
    raw_img = [times(normed_img[k], w_qkv[0]) for k in every]
    raw_txt = times(normed_txt, w_qkv[1])
    raw = [
        [(raw_img[k], s) for k in every] + [(raw_txt, k * sequences + s) for k in every]
        for s in both
    ]
    attended, norms = [], []
    order = Order()
    for s in both:
        values, norm = attend(raw[s], order(gains)[0], live_lanes, s, img_total, groups)
        attended.append(values)
        norms.append(norm)
        order.mark(norm)

    def advance(land, send):
        for red in land:
            if red.came is not None:
                red.came = order(red.came)[0]
                red.land()
                order.mark(*(red.terms if red.bit == shards else [red.away]))
        for red in send:
            if red.bit < shards:
                order.mark(red.away)
                red.send()

    def to_members(parts):
        return [parts[0]] + [shift_seq(parts[k], -k) for k in range(1, members)]

    came_attended = [to_members(attended[s][:members]) for s in both]
    came_attended_txt = [to_members(attended[s][members:]) for s in both]

    came_attended[0] = order(*came_attended[0])
    ready = gate(came_attended[0][0], *order(*img_cots[1:], *txt_cots[1:]))[1:]
    img_cots, txt_cots = [img_cots[0], *ready[: members - 1]], [txt_cots[0], *ready[members - 1 :]]
    mlp_img = [(pieces[0][5] * values.astype(F32)).astype(BF16) for values in img_cots]
    txt_grads = jnp.concatenate(txt_cots, axis=0).astype(F32) * live_rows
    mlp_txt = (text_all(pieces[1][5]) * txt_grads).astype(BF16)
    order.mark(*mlp_img, mlp_txt)

    vectors = [[p[s : s + 1] for p in pieces[0]] for s in both] + [pieces[1]]
    kinds = [0] * sequences + [1]
    units = range(sequences + 1)
    text = sequences

    def own_in():
        img, txt = order(img_in, txt_in)
        return [img[s : s + 1].astype(F32) for s in both] + [txt.astype(F32)]

    def own_grad():
        img, txt = order(img_cot, txt_cot)
        return [img[s : s + 1].astype(F32) for s in both] + [txt.astype(F32) * text_rows]

    def heads_together(parts):
        parts = [part[..., :head_width] for part in parts]
        return jnp.roll(jnp.concatenate(parts, axis=-1), member * head_width, axis=-1)

    own_attended, middle, branch, mid_stats, normed_mid = [], [], [], [], []
    tokens = own_in()
    for u in units:
        t = kinds[u]
        if t == 0:
            own_attended.append(heads_together(order(*came_attended[u])))
        else:
            parts = order(*[part for parts in came_attended_txt for part in parts])
            parts = [parts[s * members : (s + 1) * members] for s in both]
            own_attended.append(
                jnp.concatenate([heads_together(parts[s]) for s in both], axis=0)
            )
        branch.append(times(own_attended[u], w_proj[t]))
        middle.append(tokens[u] + vectors[u][2] * branch[u])
        mid_stats.append(statistics(middle[u]))
        normed = modulated(middle[u], mid_stats[u], vectors[u][3], vectors[u][4])
        order.mark(normed)
        normed_mid.append(gather_seq(normed))

    mlp_pieces = [[(mlp_img[k], s) for k in every] for s in both]
    mlp_pieces.append([(mlp_txt.reshape(1, -1, width), 0)])

    def reduction(lefts, rights):
        red = Reduction(weight_sum(lefts, rights, shards, own_bit))
        order.mark(red.away)
        return red

    def scattered(lefts, rights):
        summed = weight_sum(lefts, rights, shards)[0]
        order.mark(summed)
        return lax.psum_scatter(summed, "fsdp", scatter_dimension=0, tiled=True)[0, 0]

    def at_first(arrays):
        return [(array, 0) for array in arrays]

    def of(lists, t):
        return [array for u in units if kinds[u] == t for array in lists[u]]

    def to_owners(products):
        return [shift_seq(p.astype(BF16), -k) for k, p in enumerate(products, 1)]

    def text_members(products):
        return jnp.split(products.reshape(-1, padded, width), members, axis=0)

    active, hidden_grad = [None] * len(units), [None] * len(units)
    came_mid = [None] * len(units)
    own_text = {}

    def feed(u):
        t = kinds[u]
        normed_mid[u] = order(*normed_mid[u])
        if t == 1:
            normed_mid[u] = [jnp.concatenate(normed_mid[u], axis=0).reshape(1, -1, width)]
        active[u], hidden_grad[u] = feed_forward(
            at_first(normed_mid[u]), mlp_pieces[u], w_fc1, w_fc2, t
        )
        if t == 0:
            products = [times_t(values, w_fc1[t]).astype(BF16) for values in hidden_grad[u][1:]]
            order.mark(*products)
        else:
            parts = text_members(times_t(hidden_grad[u][0], w_fc1[t]))
            own_text["mid"], products = parts[0], parts[1:]
            order.mark(parts[0])
        came_mid[u] = to_owners(products)

    for u in [*both, text]:
        normed_mid[u] = order(*normed_mid[u])
    order.mark(*[values for u in units for values in normed_mid[u][1:]])
    feed(text)
    ready = order(active[text][0], hidden_grad[text][0])
    fc2_txt = scattered(at_first(ready[:1]), mlp_pieces[text])
    fc1_txt = scattered(at_first(normed_mid[text]), at_first(ready[1:]))
    for s in both:
        feed(s)
    active[0][0] = order(active[0][0])[0]
    fc2_img = scattered(
        at_first(of(active, 0)), [p for u in units if kinds[u] == 0 for p in mlp_pieces[u]]
    )

    middle_grad, late_grads, head_grads, branch_grad = {}, {}, {}, {}
    grads_now = own_grad()
    for u in [0, text, *range(1, sequences)]:
        t = kinds[u]
        came = order(*came_mid[u])
        if t == 0:
            mid_grad = times_t(hidden_grad[u][0], w_fc1[t])
        else:
            mid_grad = own_text["mid"]
        for values in came:
            mid_grad = mid_grad + values.astype(F32)
        average, root = mid_stats[u]
        unit = (middle[u] - average) * root
        scale_mlp_grad = jnp.sum(mid_grad * unit, axis=1)
        shift_mlp_grad = jnp.sum(mid_grad, axis=1)
        total = grads_now[u] + norm_back(mid_grad * (1.0 + vectors[u][4]), unit, root)
        middle_grad[u] = total
        gate_attn_grad = jnp.sum(total * branch[u], axis=1)
        late_grads[u] = [gate_attn_grad, shift_mlp_grad, scale_mlp_grad]
        branch_grad[u] = (vectors[u][2] * total).astype(BF16)
        attended_grad = times_t(branch_grad[u], w_proj[t]).astype(BF16)
        attended_grad = jnp.roll(attended_grad, -member * head_width, axis=-1)
        parts = []
        for k in every:
            part = attended_grad[..., k * head_width : (k + 1) * head_width]
            if head_padded > head_width:
                part = jnp.pad(part, ((0, 0), (0, 0), (0, head_padded - head_width)))
            parts.append(part)
        order.mark(*parts)
        head_grads[u] = [shift_seq(part, k) if k else part for k, part in enumerate(parts)]
    ready = order(branch_grad[text], branch_grad[0])
    branch_grad[text], branch_grad[0] = ready
    halves = None
    for t in range(2):
        halves = weight_sum(
            at_first([own_attended[u].reshape(1, -1, width) for u in units if kinds[u] == t]),
            at_first([branch_grad[u].reshape(1, -1, width) for u in units if kinds[u] == t]),
            shards,
            before=halves,
            place=t,
            places=2,
        )
    order.mark(*halves)
    proj_both = lax.psum_scatter(halves[0], "fsdp", scatter_dimension=0, tiled=True)[0]
    hidden_grad[0][0] = order(hidden_grad[0][0])[0]
    fc1_img = reduction(at_first(of(normed_mid, 0)), at_first(of(hidden_grad, 0)))
    advance([], [fc1_img])
    grads = [
        [head_grads[s][k] for k in every] + [head_grads[text][k][s : s + 1] for k in every]
        for s in both
    ]
    def finish(reds):
        while reds:
            advance(reds, reds)
            reds = [red for red in reds if red.bit < shards]

    def send_rows(values):
        blocks = values.reshape((members, -1) + values.shape[1:])
        own = pick(blocks, member, 0)
        parts = [pick(blocks, (member + k) % members, 0) for k in range(1, members)]
        order.mark(own, *parts)
        return [own] + [shift_seq(part, k) for k, part in enumerate(parts, 1)]

    def by_place(parts):
        stacked = jnp.stack(parts)
        return [pick(stacked, (member - i) % members, 0) for i in every]

    gain_parts, raw_grads, came_in, came_mlp = [], [], [], []
    for u in units:
        values = order(*active[u])
        active[u] = values
        if kinds[u] == 0:
            products = [times(v, w_fc2[0]).astype(BF16) for v in values[1:]]
            order.mark(*products)
        else:
            parts = text_members(times(values[0], w_fc2[1]))
            own_text["mlp"], products = parts[0], parts[1:]
            order.mark(parts[0])
        came_mlp.append(to_owners(products))
    advance([fc1_img], [fc1_img])

    def in_products(s):
        values = order(*raw_grads[s][1:members])
        products = [times_t(v, w_qkv[0]).astype(BF16) for v in values]
        order.mark(*products)
        return to_owners(products)

    for s in both:
        before = None
        for group in range(groups):
            before, gain_part = attend_back(
                raw[s],
                grads[s],
                attended[s],
                norms[s],
                order(gains)[0],
                live_lanes,
                s,
                img_total,
                groups,
                group,
                before,
            )
            gain_parts.append(gain_part)
            order.mark(gain_part)
            if (s, group) in ((sequences - 1, 0), (sequences - 1, groups - 1)):
                advance([fc1_img], [fc1_img])
            if (s, group) == (sequences - 1, 0):
                came_mlp = [order(*came) for came in came_mlp]
                order.mark(*[values for came in came_mlp for values in came])
            if (s, group) == (sequences - 1, 0):
                fc1_txt = send_rows(order(fc1_txt)[0].astype(F32))
        raw_grads.append(before)
        if s == 0:
            advance([fc1_img], [fc1_img])
        if s < sequences - 1:
            came_in.append(in_products(s))
    came_in = [order(*came) for came in came_in]
    fc2_img, fc2_txt = order(fc2_img, fc2_txt)
    fc1_txt = [fc1_txt[0], *order(*fc1_txt[1:])]
    order.mark(fc2_img, fc2_txt)
    order.mark(*[values for came in came_in for values in came], *fc1_txt)
    values = order(*raw_grads[-1][:members])
    raw_grads[-1] = [*values, *raw_grads[-1][members:]]
    qkv_img = reduction(
        [(normed_img[k], s) for s in both for k in every],
        at_first([raw_grads[s][k] for s in both for k in every]),
    )
    advance([], [qkv_img])
    came_in.append(in_products(sequences - 1))
    advance([qkv_img], [qkv_img])
    raw_text = jnp.concatenate([raw_grads[s][members + k] for k in every for s in both], axis=0)
    raw_text = order(raw_text)[0]
    qkv_txt = reduction(
        at_first([normed_txt.reshape(1, -1, width)]), at_first([raw_text.reshape(1, -1, triple)])
    )
    advance([], [qkv_txt])
    raw_text = order(raw_text)[0]
    parts = text_members(times_t(raw_text, w_qkv[1]))
    own_text["in"] = parts[0]
    came_in.append(to_owners(parts[1:]))
    order.mark(parts[0])
    in_grads, in_sums, outs, gate_sums = {}, {}, {}, {}
    tokens = own_in()

    def input_back(u):
        came = order(*came_in[u])
        in_grad = times_t(raw_grads[u][0], w_qkv[0]) if kinds[u] == 0 else own_text["in"]
        for values in came:
            in_grad = in_grad + values.astype(F32)
        average, root = statistics(tokens[u])
        unit = (tokens[u] - average) * root
        in_sums[u] = [jnp.sum(in_grad, axis=1), jnp.sum(in_grad * unit, axis=1)]
        in_grads[u] = middle_grad[u] + norm_back(in_grad * (1.0 + vectors[u][1]), unit, root)
        order.mark(in_grads[u], *in_sums[u])

    def output(u):
        came = order(*came_mlp[u])
        mlp_out = times(active[u][0], w_fc2[0]) if kinds[u] == 0 else own_text["mlp"]
        for values in came:
            mlp_out = mlp_out + values.astype(F32)
        result = middle[u] + vectors[u][5] * mlp_out
        if kinds[u] == 1:
            result = result * text_rows
        outs[u] = result.astype(BF16)
        gate_sums[u] = jnp.sum(grads_late[u] * mlp_out, axis=1)
        order.mark(outs[u], gate_sums[u])

    grads_late = own_grad()
    output(0)
    advance([qkv_txt], [qkv_txt])
    proj_both = order(proj_both)[0]
    order.mark(proj_both)
    advance([qkv_img], [qkv_img])
    input_back(sequences - 1)
    advance([qkv_img], [qkv_img])
    input_back(text)
    for s in range(sequences - 1):
        input_back(s)
    advance([qkv_txt], [qkv_txt])
    for u in units:
        if u:
            output(u)
    mod_rows = [
        jnp.concatenate([*in_sums[u], *late_grads[u], gate_sums[u]], axis=-1) for u in units
    ]
    img_out = jnp.concatenate([outs[s] for s in both], axis=0)
    txt_out = outs[text][:, :slots]
    img_grad = jnp.concatenate([in_grads[s] for s in both], axis=0)
    txt_grad = in_grads[text][:, :slots]

    gain_own = sum(jnp.sum(part, axis=0) for part in gain_parts)[:4]
    gain_own = (gain_own[:, :HEAD] + gain_own[:, HEAD:]).reshape(-1)
    mod_own = jnp.stack([jnp.concatenate(mod_rows[:-1], axis=0), mod_rows[-1]], axis=1)
    mod_count = mod_own.size
    own_shared = jnp.concatenate([mod_own.reshape(-1), gain_own])
    order.mark(own_shared)
    came_shared = gather_seq(own_shared)[1:]
    finish([fc1_img])
    finish([qkv_img])
    ready = order(fc2_img, fc2_txt)
    order.mark(*ready)
    qkv_rows = send_rows(qkv_img.result()[0])
    shared = sum(order(*came_shared), own_shared)
    gain_high = shared[mod_count:].astype(BF16)
    gain_low = (shared[mod_count:] - gain_high.astype(F32)).astype(BF16)
    packed = jnp.concatenate([shared[:mod_count].astype(BF16), gain_high, gain_low])
    packed = jnp.broadcast_to(packed.reshape(1, -1, LANES), (shards, packed.size // LANES, LANES))
    order.mark(packed)
    packed = lax.all_to_all(packed, "fsdp", split_axis=0, concat_axis=0, tiled=True)
    advance([qkv_txt], [qkv_txt])

    ready = order(*ready)
    fc2_grad = jnp.stack(ready[:2]).astype(F32)
    fc1_rows = send_rows(fc1_img.result()[0])
    proj_rows = send_rows(jnp.transpose(proj_both.astype(F32), (1, 0, 2)))

    def heads_apart(parts):
        parts = by_place(parts)
        return jnp.concatenate(
            [
                parts[m][:, (g * 3 + part) * group_width :][
                    :, : min(group_width, head_width - g * group_width)
                ]
                for part in range(3)
                for m in every
                for g in range(groups)
            ],
            axis=1,
        )

    qkv_rows = [qkv_rows[0], *order(*qkv_rows[1:])]
    image_grad = heads_apart(qkv_rows)
    order.mark(image_grad, fc2_grad)

    packed = order(packed)[0]
    mod_lanes = mod_count // LANES
    every_mod = packed[:, :mod_lanes].reshape(shards * sequences, 2, mod_width)
    gain_grad = jnp.sum(packed[:, mod_lanes:].astype(F32), axis=0)
    gain_grad = gain_grad.reshape(2, 2, 2 * HEAD).sum(axis=0)
    cond_part = jnp.einsum("stm,tdm->sd", every_mod, ada_w, preferred_element_type=F32)
    order.mark(cond_part)
    cond_full = lax.all_to_all(cond_part, "fsdp", split_axis=0, concat_axis=1, tiled=True)
    finish([qkv_txt])
    text_rows_sent = send_rows(qkv_txt.result()[0])
    every_mod = order(every_mod)[0]
    out_rows = width // (shards * members)
    own_cols = lax.dynamic_slice_in_dim(cond_cols, member * out_rows, out_rows, 1)
    ada_grad = jnp.einsum("sr,stm->trm", own_cols, every_mod, preferred_element_type=F32)
    proj_grad = jnp.transpose(sum(order(*proj_rows[1:]), proj_rows[0]), (1, 0, 2))
    fc1_rows = [fc1_rows[0], *order(*fc1_rows[1:])]
    fc1_grad = jnp.stack([join_units(by_place(rows), shards) for rows in (fc1_rows, fc1_txt)])
    order.mark(ada_grad, proj_grad, fc1_grad)
    cond_grad = jax.vjp(jax.nn.silu, cond.astype(F32))[1](order(cond_full)[0])[0]
    text_grad = heads_apart([text_rows_sent[0], *order(*text_rows_sent[1:])])
    qkv_grad = jnp.stack([image_grad, text_grad])
    return (
        img_out,
        txt_out,
        img_grad,
        txt_grad,
        cond_grad,
        ada_grad,
        qkv_grad,
        proj_grad,
        fc1_grad,
        fc2_grad,
        gain_grad,
    )


def solution(mesh):
    tokens, rows = P("fsdp", "seq", None), P("fsdp", None)
    weight, weight_grad = P(None, "fsdp", None), P(None, ("fsdp", "seq"), None)
    in_specs = (tokens, tokens, rows, rows) + (weight,) * 5 + (P(), tokens, tokens)
    out_specs = (tokens,) * 4 + (rows,) + (weight_grad,) * 5 + (P(),)
    return jax.shard_map(body, mesh=mesh, in_specs=in_specs, out_specs=out_specs, check_vma=False)
```

```python
import math

import jax
import jax.numpy as jnp
from jax import lax
from jax.experimental import pallas as pl
from jax.experimental.pallas import tpu as pltpu
from jax.sharding import PartitionSpec as P

HEAD = 64
LANES = 128
BLOCK = 1024
BF16 = jnp.bfloat16
F32 = jnp.float32
SCALE = HEAD**-0.5
SCALE2 = SCALE * math.log2(math.e)
VMEM_LIMIT = 56 * 1024 * 1024
NT = (((1,), (1,)), ((), ()))
NN = (((1,), (0,)), ((), ()))


def dot(left, right, dims=NN):
    return lax.dot_general(left, right, dims, preferred_element_type=F32)


def low_lanes():
    return lax.broadcasted_iota(jnp.int32, (1, LANES), 1) < HEAD


def head_mean(values):
    low = low_lanes()
    first = jnp.sum(jnp.where(low, values, 0.0), axis=-1, keepdims=True)
    second = jnp.sum(jnp.where(low, 0.0, values), axis=-1, keepdims=True)
    return jnp.where(low, first, second) * (1.0 / HEAD)


def rms(values):
    return lax.rsqrt(head_mean(values * values) + 1e-06)


def blocks_of(total, size):
    return [(start, min(size, total - start)) for start in range(0, total, size)]


def attend_kernel(rows, img_total, *refs):
    count = len(rows)
    raw, refs = refs[: 3 * count], refs[3 * count :]
    gain_ref, live_ref = refs[:2]
    out, refs = refs[2 : 2 + count], refs[2 + count :]
    norm_ref, q_s, k0_s, k1_s, v0_s, v1_s, o_s = refs
    low = low_lanes()
    offset = 0
    for i, size in enumerate(rows):
        text = offset >= img_total
        place = pl.ds(offset, size)
        gain = 2 if text else 0
        query, key, value = (raw[3 * i + part][0] for part in range(3))
        q_s[place, :] = (query * rms(query) * gain_ref[gain : gain + 1, :]).astype(BF16)
        key = key * rms(key) * gain_ref[gain + 1 : gain + 2, :]
        k0_s[place, :] = jnp.where(low, key, 0.0).astype(BF16)
        k1_s[place, :] = jnp.where(low, 0.0, key).astype(BF16)
        if text:
            live = live_ref[0, pl.ds(offset - img_total, size), :]
            value = value * live
        else:
            live = jnp.ones_like(value)
        v0_s[place, :] = jnp.where(low, value, live).astype(BF16)
        v1_s[place, :] = jnp.where(low, live, value).astype(BF16)
        offset += size

    def block(start, size):
        place = pl.ds(start, size)
        query = q_s[place, :]
        sums = []
        for key_ref, value_ref in ((k0_s, v0_s), (k1_s, v1_s)):
            weights = jnp.exp2(dot(query, key_ref[...], NT) * SCALE2).astype(BF16)
            sums.append(dot(weights, value_ref[...]))
        top = jnp.where(low, sums[0], sums[1])
        bottom = pltpu.roll(jnp.where(low, sums[1], sums[0]), HEAD, 1)
        o_s[place, :] = (top / bottom).astype(BF16)
        turned = jnp.log2(bottom).T
        norm_ref[0, 0, 0:8, place] = turned[0:8]
        norm_ref[0, 0, 8:16, place] = turned[HEAD : HEAD + 8]

    def step(i, carry):
        block(pl.multiple_of(i * BLOCK, BLOCK), BLOCK)
        return carry

    lax.fori_loop(0, img_total // BLOCK, step, 0)
    for start, size in blocks_of(offset - img_total, BLOCK):
        block(img_total + start, size)
    offset = 0
    for i, size in enumerate(rows):
        out[i][0] = o_s[pl.ds(offset, size), :]
        offset += size


def attend_back_kernel(rows, img_total, width, *refs):
    count = len(rows)
    raw, refs = refs[: 3 * count], refs[3 * count :]
    grad, refs = refs[:count], refs[count:]
    done, refs = refs[:count], refs[count:]
    norm_ref, gain_ref, live_ref = refs[:3]
    out, refs = refs[3 : 3 + count], refs[3 + count :]
    gain_out, q_s, k_s, v_s, kt_s, do_s, o_s, dq_s, dk_s, dv_s = refs
    low = low_lanes()
    pair = pl.program_id(0)
    offset = 0
    for i, size in enumerate(rows):
        text = offset >= img_total
        place = pl.ds(offset, size)
        gain = 2 if text else 0
        query, key, value = (raw[3 * i + part][0] for part in range(3))
        q_s[place, :] = (query * rms(query) * gain_ref[gain : gain + 1, :]).astype(BF16)
        key = (key * rms(key) * gain_ref[gain + 1 : gain + 2, :]).astype(BF16)
        k_s[place, :] = key
        v_s[place, :] = value.astype(BF16)
        do_s[place, :] = grad[i][0]
        o_s[place, :] = done[i][0]
        offset += size
    total = offset
    key_blocks = blocks_of(img_total, BLOCK) + [
        (img_total + start, size) for start, size in blocks_of(total - img_total, BLOCK)
    ]
    for start, size in key_blocks:
        key = k_s[pl.ds(start, size), :].astype(F32)
        if start >= img_total:
            key = key * live_ref[0, pl.ds(start - img_total, size), :]
        kt_s[:, pl.ds(start, size)] = key.T.astype(BF16)
    dk_s[...] = jnp.zeros_like(dk_s)
    dv_s[...] = jnp.zeros_like(dv_s)

    def block(start, size):
        place = pl.ds(start, size)
        query = q_s[place, :]
        grads = do_s[place, :]
        both = (grads.astype(F32) * o_s[place, :].astype(F32)).T
        side = []
        for h in range(2):
            delta = jnp.sum(both[h * HEAD : (h + 1) * HEAD], axis=0, keepdims=True)
            norm = norm_ref[0, 0, 8 * h : 8 * h + 1, place]
            own = low if h == 0 else jnp.logical_not(low)
            query_h = jnp.where(own, query, jnp.zeros_like(query))
            grads_h = jnp.where(own, grads, jnp.zeros_like(grads))
            side.append((delta, norm, query_h, grads_h))
        probs, changes = [], []
        for delta, norm, query_h, grads_h in side:
            prob = jnp.exp2(dot(k_s[...], query_h, NT) * SCALE2 - norm)
            prob_grad = dot(v_s[...], grads_h, NT)
            changes.append((prob * (prob_grad - delta)).astype(BF16))
            probs.append(prob.astype(BF16))
        dv_s[...] += dot(probs[0], side[0][3]) + dot(probs[1], side[1][3])
        dk_s[...] += dot(changes[0], side[0][2]) + dot(changes[1], side[1][2])
        turned = [dot(kt_s[h * HEAD : (h + 1) * HEAD, :], changes[h]) for h in range(2)]
        dq_s[place, :] = jnp.concatenate(turned, axis=0).T

    def step(i, carry):
        block(pl.multiple_of(i * BLOCK, BLOCK), BLOCK)
        return carry

    lax.fori_loop(0, img_total // BLOCK, step, 0)
    for start, size in blocks_of(total - img_total, BLOCK):
        block(img_total + start, size)

    gain_sums = [jnp.zeros((1, LANES), F32) for _ in range(4)]
    offset = 0
    for i, size in enumerate(rows):
        text = offset >= img_total
        place = pl.ds(offset, size)
        value_grad = dv_s[place, :]
        key_grad = dk_s[place, :]
        if text:
            live = live_ref[0, pl.ds(offset - img_total, size), :]
            value_grad = value_grad * live
            key_grad = key_grad * live
        for part, change in enumerate((dq_s[place, :], key_grad)):
            row = (2 if text else 0) + part
            change = (change * SCALE).astype(BF16).astype(F32)
            values = raw[3 * i + part][0]
            root = rms(values)
            unit = values * root
            gain_sums[row] += jnp.sum(change * unit, axis=0, keepdims=True)
            change = change * gain_ref[row : row + 1, :]
            change = root * (change - unit * head_mean(change * unit))
            column = pl.multiple_of(part * width + pair * LANES, LANES)
            out[i][0, :, pl.ds(column, LANES)] = change.astype(BF16)
        column = pl.multiple_of(2 * width + pair * LANES, LANES)
        out[i][0, :, pl.ds(column, LANES)] = value_grad.astype(BF16)
        offset += size
    for row in range(4):
        gain_out[0, row : row + 1, :] = gain_sums[row]
    gain_out[0, 4:8, :] = jnp.zeros((4, LANES), F32)


def cost(flops, bytes_accessed, transcendentals=0):
    return pl.CostEstimate(
        flops=flops, bytes_accessed=bytes_accessed, transcendentals=transcendentals
    )


PARAMS = pltpu.CompilerParams(vmem_limit_bytes=VMEM_LIMIT)


def raw_specs(raw, group, count):
    return [
        pl.BlockSpec(
            (1, array.shape[1], LANES),
            lambda p, sel=sel, part=part: (sel, 0, (group * 3 + part) * count + p),
        )
        for array, sel in raw
        for part in range(3)
    ]


def rows_of(pieces):
    return [array.shape[1] for array, _ in pieces]


def attend(raw, gains, live, sequence, img_total, groups):
    width = raw[0][0].shape[2] // 3
    pairs = width // LANES
    count = pairs // groups
    rows = rows_of(raw)
    total = sum(rows)

    def kernel(*refs):
        attend_kernel(rows, img_total, *refs)

    work = pairs * 2 * total * total
    outputs = pl.pallas_call(
        kernel,
        grid=(pairs,),
        in_specs=[
            pl.BlockSpec(
                (1, array.shape[1], LANES),
                lambda p, sel=sel, part=part: (
                    sel,
                    0,
                    (p // count * 3 + part) * count + p % count,
                ),
            )
            for array, sel in raw
            for part in range(3)
        ]
        + [
            pl.BlockSpec((4, LANES), lambda p: (0, 0)),
            pl.BlockSpec((1, total - img_total, LANES), lambda p: (sequence, 0, 0)),
        ],
        out_specs=[pl.BlockSpec((1, size, LANES), lambda p: (0, 0, p)) for size in rows]
        + [pl.BlockSpec((1, 1, 16, total), lambda p: (0, p, 0, 0))],
        out_shape=[jax.ShapeDtypeStruct((1, size, width), BF16) for size in rows]
        + [jax.ShapeDtypeStruct((1, pairs, 16, total), F32)],
        scratch_shapes=[pltpu.VMEM((total, LANES), BF16)] * 6,
        compiler_params=PARAMS,
        cost_estimate=cost(work * 4 * LANES, total * width * 14, work),
        name="attend",
    )(*[array for array, _ in raw for _ in range(3)], gains, live)
    return (list(outputs[:-1]), outputs[-1])


def attend_back(raw, grads, done, norm, gains, live, sequence, img_total, groups, group, before):
    triple = raw[0][0].shape[2]
    width = triple // 3
    pairs = width // LANES
    count = pairs // groups
    rows = rows_of(raw)
    total = sum(rows)
    pieces = len(rows)

    def kernel(*refs):
        if before is not None:
            refs = refs[pieces:]
        attend_back_kernel(rows, img_total, count * LANES, *refs)

    head_specs = [
        pl.BlockSpec((1, size, LANES), lambda p: (0, 0, group * count + p)) for size in rows
    ]
    in_specs = (
        raw_specs(raw, group, count)
        + head_specs
        + head_specs
        + [
            pl.BlockSpec((1, 1, 16, total), lambda p: (0, group * count + p, 0, 0)),
            pl.BlockSpec((4, LANES), lambda p: (0, 0)),
            pl.BlockSpec((1, total - img_total, LANES), lambda p: (sequence, 0, 0)),
        ]
    )
    operands = [array for array, _ in raw for _ in range(3)]
    operands += [*grads, *done, norm, gains, live]
    aliases = {}
    if before is not None:
        in_specs = [pl.BlockSpec(memory_space=pl.ANY)] * pieces + in_specs
        operands = list(before) + operands
        aliases = {i: i for i in range(pieces)}
    work = count * 2 * total * total
    outputs = pl.pallas_call(
        kernel,
        grid=(count,),
        in_specs=in_specs,
        out_specs=[
            pl.BlockSpec((1, size, 3 * count * LANES), lambda p: (0, 0, group)) for size in rows
        ]
        + [pl.BlockSpec((1, 8, LANES), lambda p: (p, 0, 0))],
        out_shape=[jax.ShapeDtypeStruct((1, size, triple), BF16) for size in rows]
        + [jax.ShapeDtypeStruct((count, 8, LANES), F32)],
        scratch_shapes=[pltpu.VMEM((total, LANES), BF16)] * 3
        + [pltpu.VMEM((LANES, total), BF16)]
        + [pltpu.VMEM((total, LANES), BF16)] * 2
        + [pltpu.VMEM((total, LANES), F32)] * 3,
        compiler_params=PARAMS,
        input_output_aliases=aliases,
        cost_estimate=cost(work * 10 * LANES, total * count * LANES * 22, work),
        name="attend_back",
    )(*operands)
    return (list(outputs[:-1]), outputs[-1])


def tile_of(extent):
    for size in (1024, 768, 512, 384, 256, 128):
        if extent % size == 0:
            return size
    return extent


def feed_forward(values, grads, weight_in, weight_out, modality):
    width = weight_out.shape[2]
    units = weight_out.shape[1]
    tile = tile_of(units)
    rows = rows_of(values)
    count = len(rows)

    def kernel(*refs):
        in_ref, out_ref = refs[2 * count : 2 * count + 2]
        slope = math.sqrt(2 / math.pi)
        for i in range(count):
            value = dot(refs[i][0], in_ref[0])
            grad = dot(refs[count + i][0], out_ref[0], NT)
            square = value * value
            bent = jnp.tanh(value * (slope + (slope * 0.044715) * square))
            half = 0.5 * value
            rise = 0.5 + 0.5 * bent
            refs[2 * count + 2 + i][0] = (value * rise).astype(BF16)
            rise = rise + half * (1.0 - bent * bent) * (slope + (3 * slope * 0.044715) * square)
            refs[3 * count + 2 + i][0] = (grad * rise).astype(BF16)

    total = sum(rows)
    outputs = pl.pallas_call(
        kernel,
        grid=(units // tile,),
        in_specs=[
            pl.BlockSpec((1, size, width), lambda j, sel=sel: (sel, 0, 0))
            for (_, sel), size in zip(list(values) + list(grads), rows * 2)
        ]
        + [
            pl.BlockSpec((1, width, tile), lambda j: (modality, 0, j)),
            pl.BlockSpec((1, tile, width), lambda j: (modality, j, 0)),
        ],
        out_specs=[pl.BlockSpec((1, size, tile), lambda j: (0, 0, j)) for size in rows] * 2,
        out_shape=[jax.ShapeDtypeStruct((1, size, units), BF16) for size in rows] * 2,
        compiler_params=PARAMS,
        cost_estimate=cost(
            4 * total * width * units, total * 4 * (width + units) + 4 * units * width, total * units
        ),
        name="feed_forward",
    )(*[a for a, _ in values], *[a for a, _ in grads], weight_in, weight_out)
    return (list(outputs[:count]), list(outputs[count:]))


def weight_sum(lefts, rights, blocks, bit=None, before=None, place=0, places=1):
    rows = lefts[0][0].shape[2]
    columns = rights[0][0].shape[2]
    block = rows // blocks
    row_tile = max(size for size in (768, 512, 384, rows) if rows % size == 0 and size % (2 * block) == 0)
    tile = tile_of(columns)
    sizes = rows_of(lefts)
    count = len(sizes)
    run = row_tile // block

    def kernel(*refs):
        bit_ref, refs = refs[0], refs[len(first) :]
        total = None
        for i in range(count):
            part = lax.dot_general(
                refs[i][0], refs[count + i][0], (((0,), (0,)), ((), ())), preferred_element_type=F32
            )
            total = part if total is None else total + part
        if bit is None:
            for j in range(run):
                refs[2 * count][j, 0] = total[j * block : (j + 1) * block].astype(BF16)
        else:
            keep_ref, away_ref = refs[2 * count :]
            odd = bit_ref[0] == 1
            for j in range(run // 2):
                even_rows = total[2 * j * block : (2 * j + 1) * block]
                odd_rows = total[(2 * j + 1) * block : (2 * j + 2) * block]
                keep_ref[j, 0] = jnp.where(odd, odd_rows, even_rows).astype(BF16)
                away_ref[j, 0] = jnp.where(odd, even_rows, odd_rows).astype(BF16)

    total = sum(sizes)
    if bit is None:
        arrays, divide = 1, 1
    else:
        arrays, divide = 2, 2
    out_shape = [jax.ShapeDtypeStruct((blocks // divide, places, block, columns), BF16)] * arrays
    out_specs = [
        pl.BlockSpec((run // divide, 1, block, tile), lambda i, j: (i, place, 0, j))
    ] * arrays
    first_specs, first, aliases = [], [], {}
    if bit is not None:
        first_specs, first = [pl.BlockSpec(memory_space=pltpu.SMEM)], [bit]
    if before is not None:
        aliases = {len(first) + i: i for i in range(arrays)}
        first_specs = first_specs + [pl.BlockSpec(memory_space=pl.ANY)] * arrays
        first = first + list(before)
    return pl.pallas_call(
        kernel,
        grid=(rows // row_tile, columns // tile),
        in_specs=first_specs
        + [
            pl.BlockSpec((1, size, row_tile), lambda i, j, sel=sel: (sel, 0, i))
            for (_, sel), size in zip(lefts, sizes)
        ]
        + [
            pl.BlockSpec((1, size, tile), lambda i, j, sel=sel: (sel, 0, j))
            for (_, sel), size in zip(rights, sizes)
        ],
        out_specs=out_specs,
        out_shape=out_shape,
        compiler_params=PARAMS,
        input_output_aliases=aliases,
        cost_estimate=cost(
            2 * total * rows * columns, 2 * (total * (rows + columns) + rows * columns)
        ),
        name="weight_sum",
    )(*first, *[a for a, _ in lefts], *[a for a, _ in rights])


def pick_heads(weight, other, member, members, groups, group_width):
    rows, columns = weight.shape
    width = columns // 3
    head_width = width // members
    size = lambda group: min(group_width, head_width - group * group_width)

    def kernel(member_ref, in_ref, other_ref, out_ref):
        for m in range(members):

            @pl.when(member_ref[0] == m)
            def _():
                for group in range(groups):
                    for part in range(3):
                        start = part * width + m * head_width + group * group_width
                        piece = in_ref[:, start : start + size(group)]
                        if size(group) < group_width:
                            blank = jnp.zeros((rows, group_width - size(group)), piece.dtype)
                            piece = jnp.concatenate([piece, blank], axis=1)
                        place = (group * 3 + part) * group_width
                        out_ref[:, place : place + group_width] = piece

        out_ref[:, 3 * groups * group_width :] = other_ref[...]

    total = 3 * groups * group_width + other.shape[1]
    return pl.pallas_call(
        kernel,
        in_specs=[pl.BlockSpec(memory_space=pltpu.SMEM)]
        + [pl.BlockSpec(memory_space=pltpu.VMEM)] * 2,
        out_specs=pl.BlockSpec(memory_space=pltpu.VMEM),
        out_shape=jax.ShapeDtypeStruct((rows, total), weight.dtype),
        compiler_params=PARAMS,
        cost_estimate=cost(0, 4 * rows * columns),
        name="pick_heads",
    )(member, weight, other)


def pick_units(weight, member, members, shards):
    rows, columns = weight.shape
    unit = columns // (shards * members)

    def kernel(member_ref, in_ref, out_ref):
        for m in range(members):

            @pl.when(member_ref[0] == m)
            def _():
                out_ref[...] = jnp.concatenate(
                    [
                        in_ref[:, (f * members + m) * unit : (f * members + m + 1) * unit]
                        for f in range(shards)
                    ],
                    axis=1,
                )

    return pl.pallas_call(
        kernel,
        in_specs=[pl.BlockSpec(memory_space=pltpu.SMEM), pl.BlockSpec(memory_space=pltpu.VMEM)],
        out_specs=pl.BlockSpec(memory_space=pltpu.VMEM),
        out_shape=jax.ShapeDtypeStruct((rows, columns // members), weight.dtype),
        compiler_params=PARAMS,
        cost_estimate=cost(0, 2 * rows * columns * 2),
        name="pick_units",
    )(member, weight)


def join_units(parts, shards):
    rows, columns = parts[0].shape
    unit = columns // shards

    def kernel(*refs):
        refs[-1][...] = jnp.concatenate(
            [ref[:, f * unit : (f + 1) * unit] for f in range(shards) for ref in refs[:-1]], axis=1
        )

    return pl.pallas_call(
        kernel,
        in_specs=[pl.BlockSpec(memory_space=pltpu.VMEM)] * len(parts),
        out_specs=pl.BlockSpec(memory_space=pltpu.VMEM),
        out_shape=jax.ShapeDtypeStruct((rows, columns * len(parts)), parts[0].dtype),
        compiler_params=PARAMS,
        cost_estimate=cost(0, 8 * rows * columns * len(parts)),
        name="join_units",
    )(*parts)


def shift_seq(values, amount):
    members = lax.axis_size("seq")
    return lax.ppermute(values, "seq", [(i, (i + amount) % members) for i in range(members)])


def gather_seq(values):
    return [values] + [shift_seq(values, k) for k in range(1, lax.axis_size("seq"))]


def pick(values, index, axis):
    return lax.dynamic_index_in_dim(values, index, axis, keepdims=False)


class Reduction:
    def __init__(self, halves):
        self.terms, self.away = [halves[0]], halves[1]
        self.bit, self.came = 1, None

    def send(self):
        size = lax.axis_size("fsdp")
        self.came = lax.ppermute(self.away, "fsdp", [(i, i ^ self.bit) for i in range(size)])

    def land(self):
        self.terms.append(self.came)
        self.bit, self.came = self.bit * 2, None
        if self.bit < lax.axis_size("fsdp"):
            mine = (lax.axis_index("fsdp") // self.bit) % 2
            terms = [t.reshape((t.shape[0] // 2, 2) + t.shape[1:]) for t in self.terms]
            self.away = sum(pick(t, 1 - mine, 1).astype(F32) for t in terms).astype(BF16)
            self.terms = [pick(t, mine, 1) for t in terms]

    def result(self):
        return sum(t.astype(F32) for t in self.terms)[0]


def gate(first, *others):
    return lax.optimization_barrier((first, *others))


class Order:
    def __init__(self):
        self.marks, self.closed = [], False

    def __call__(self, *arrays):
        if not arrays:
            return []
        self.closed = True
        return list(gate(*arrays, *self.marks)[: len(arrays)])

    def mark(self, *arrays):
        if self.closed:
            self.marks, self.closed = [], False
        self.marks += arrays


def statistics(values):
    average = jnp.mean(values, axis=-1, keepdims=True)
    centred = values - average
    return (average, lax.rsqrt(jnp.mean(centred * centred, axis=-1, keepdims=True) + 1e-06))


def modulated(values, stats, shift, scale):
    return (((values - stats[0]) * stats[1]) * (1.0 + scale) + shift).astype(BF16)


def norm_back(grad, unit, root):
    return root * (
        grad
        - jnp.mean(grad, axis=-1, keepdims=True)
        - unit * jnp.mean(grad * unit, axis=-1, keepdims=True)
    )


def times(left, right):
    return lax.dot_general(left, right, (((2,), (0,)), ((), ())), preferred_element_type=F32)


def times_t(left, right):
    return lax.dot_general(left, right, (((2,), (1,)), ((), ())), preferred_element_type=F32)


def pad_rows(values, rows):
    return jnp.pad(values, ((0, 0), (0, rows - values.shape[1]), (0, 0)))


def body(
    img_in, txt_in, cond, text_counts, ada_w, qkv_w, proj_w, fc1_w, fc2_w, qk_gain, img_cot, txt_cot
):
    members = lax.axis_size("seq")
    member = lax.axis_index("seq")
    shards = lax.axis_size("fsdp")
    sequences, img_local, width = img_in.shape
    slots = txt_in.shape[1]
    padded = -(-slots // 16) * 16
    img_total = members * img_local
    head_width = width // members
    head_padded = -(-head_width // LANES) * LANES
    groups = 2 if (head_padded // LANES) % 2 == 0 else 1
    group_width = head_padded // groups
    hidden_width = fc1_w.shape[2]
    shard_rows = ada_w.shape[1]
    unit_rows = hidden_width // (shards * members)
    member_index = member.reshape(1)
    own_bit = (lax.axis_index("fsdp") % 2).reshape(1)
    every = range(members)
    both = range(sequences)

    txt_in, txt_cot = pad_rows(txt_in, padded), pad_rows(txt_cot, padded)
    img_all, txt_all = gather_seq(img_in), gather_seq(txt_in)
    ready = gate(img_cot, txt_cot, *img_all[1:])
    img_cots, txt_cots = gather_seq(ready[0]), gather_seq(ready[1])

    own_both = pick_heads(
        qkv_w.reshape(2 * shard_rows, 3 * width),
        proj_w.reshape(2 * shard_rows, width),
        member_index,
        members,
        groups,
        group_width,
    )
    w_both = lax.all_gather(own_both.reshape(2, shard_rows, -1), "fsdp", axis=1, tiled=True)
    triple = 3 * head_padded
    w_qkv = [w_both[t, :, :triple] for t in range(2)]
    w_proj = [w_both[t, :, triple:] for t in range(2)]

    cond_act = jax.nn.silu(cond.astype(F32)).astype(BF16)
    cond_cols = lax.all_to_all(
        cond_act.reshape(sequences, shards, shard_rows), "fsdp", split_axis=1, concat_axis=0, tiled=True
    ).reshape(shards * sequences, shard_rows)
    mod_width = ada_w.shape[2]
    share = mod_width // members
    own_ada = lax.dynamic_slice_in_dim(ada_w, member * share, share, 2)
    mod_part = jnp.einsum("sd,tdm->stm", cond_cols, own_ada, preferred_element_type=F32)
    mod_part = mod_part.reshape(shards, sequences, 2, share)
    mod_part, fc1_w, fc2_w = gate(mod_part, fc1_w, fc2_w)
    mod_sum = jnp.sum(
        lax.all_to_all(mod_part, "fsdp", split_axis=0, concat_axis=0, tiled=True), axis=0
    )
    mod_shares = jnp.stack(gather_seq(mod_sum))
    modulation = jnp.concatenate(
        [pick(mod_shares, (member - i) % members, 0) for i in every], axis=-1
    )

    own_fc1 = pick_units(fc1_w.reshape(2 * shard_rows, hidden_width), member_index, members, shards)
    own_fc2 = pick(fc2_w.reshape(2, members, unit_rows, width), member, 1)
    w_fc1 = lax.all_gather(own_fc1.reshape(2, shard_rows, -1), "fsdp", axis=1, tiled=True)
    w_fc2 = lax.all_gather(own_fc2, "fsdp", axis=1, tiled=True)

    counts = jnp.stack([pick(text_counts, (member - k) % members, 1) for k in every], axis=1)
    slot_ids = lax.broadcasted_iota(jnp.int32, (sequences, members, padded), 2)
    live = (slot_ids < counts[:, :, None]).astype(F32)
    live_rows = jnp.transpose(live, (1, 0, 2)).reshape(members * sequences, padded, 1)
    text_rows = live_rows[:sequences]
    live_lanes = jnp.broadcast_to(
        live.reshape(sequences, members * padded, 1), (sequences, members * padded, LANES)
    )
    gains = jnp.tile(qk_gain.reshape(4, HEAD), (1, 2))
    pieces = [
        [piece[:, None, :] for piece in jnp.split(modulation[:, t], 6, axis=-1)] for t in range(2)
    ]

    def text_all(vector):
        return jnp.tile(vector, (members, 1, 1))

    ready = gate(modulation, *img_all[1:], *txt_all[1:])
    img_all, txt_all = [img_all[0], *ready[1:members]], [txt_all[0], *ready[members:]]
    img_f32 = [values.astype(F32) for values in img_all]
    img_stats = [statistics(values) for values in img_f32]
    txt_f32 = jnp.concatenate(txt_all, axis=0).astype(F32)
    txt_stats = statistics(txt_f32)
    normed_img = [modulated(img_f32[k], img_stats[k], pieces[0][0], pieces[0][1]) for k in every]
    normed_txt = modulated(txt_f32, txt_stats, text_all(pieces[1][0]), text_all(pieces[1][1]))
    raw_img = [times(normed_img[k], w_qkv[0]) for k in every]
    raw_txt = times(normed_txt, w_qkv[1])
    raw = [
        [(raw_img[k], s) for k in every] + [(raw_txt, k * sequences + s) for k in every]
        for s in both
    ]
    attended, norms = [], []
    order = Order()
    for s in both:
        values, norm = attend(raw[s], order(gains)[0], live_lanes, s, img_total, groups)
        attended.append(values)
        norms.append(norm)
        order.mark(norm)

    def advance(land, send):
        for red in land:
            if red.came is not None:
                red.came = order(red.came)[0]
                red.land()
                order.mark(*(red.terms if red.bit == shards else [red.away]))
        for red in send:
            if red.bit < shards:
                order.mark(red.away)
                red.send()

    def to_members(parts):
        return [parts[0]] + [shift_seq(parts[k], -k) for k in range(1, members)]

    came_attended = [to_members(attended[s][:members]) for s in both]
    came_attended_txt = [to_members(attended[s][members:]) for s in both]

    came_attended[0] = order(*came_attended[0])
    ready = gate(came_attended[0][0], *order(*img_cots[1:], *txt_cots[1:]))[1:]
    img_cots, txt_cots = [img_cots[0], *ready[: members - 1]], [txt_cots[0], *ready[members - 1 :]]
    mlp_img = [(pieces[0][5] * values.astype(F32)).astype(BF16) for values in img_cots]
    txt_grads = jnp.concatenate(txt_cots, axis=0).astype(F32) * live_rows
    mlp_txt = (text_all(pieces[1][5]) * txt_grads).astype(BF16)
    order.mark(*mlp_img, mlp_txt)

    vectors = [[p[s : s + 1] for p in pieces[0]] for s in both] + [pieces[1]]
    kinds = [0] * sequences + [1]
    units = range(sequences + 1)
    text = sequences

    def own_in():
        img, txt = order(img_in, txt_in)
        return [img[s : s + 1].astype(F32) for s in both] + [txt.astype(F32)]

    def own_grad():
        img, txt = order(img_cot, txt_cot)
        return [img[s : s + 1].astype(F32) for s in both] + [txt.astype(F32) * text_rows]

    def heads_together(parts):
        parts = [part[..., :head_width] for part in parts]
        return jnp.roll(jnp.concatenate(parts, axis=-1), member * head_width, axis=-1)

    own_attended, middle, branch, mid_stats, normed_mid = [], [], [], [], []
    tokens = own_in()
    for u in units:
        t = kinds[u]
        if t == 0:
            own_attended.append(heads_together(order(*came_attended[u])))
        else:
            parts = order(*[part for parts in came_attended_txt for part in parts])
            parts = [parts[s * members : (s + 1) * members] for s in both]
            own_attended.append(
                jnp.concatenate([heads_together(parts[s]) for s in both], axis=0)
            )
        branch.append(times(own_attended[u], w_proj[t]))
        middle.append(tokens[u] + vectors[u][2] * branch[u])
        mid_stats.append(statistics(middle[u]))
        normed = modulated(middle[u], mid_stats[u], vectors[u][3], vectors[u][4])
        order.mark(normed)
        normed_mid.append(gather_seq(normed))

    mlp_pieces = [[(mlp_img[k], s) for k in every] for s in both]
    mlp_pieces.append([(mlp_txt.reshape(1, -1, width), 0)])

    def reduction(lefts, rights):
        red = Reduction(weight_sum(lefts, rights, shards, own_bit))
        order.mark(red.away)
        return red

    def scattered(lefts, rights):
        summed = weight_sum(lefts, rights, shards)[0]
        order.mark(summed)
        return lax.psum_scatter(summed, "fsdp", scatter_dimension=0, tiled=True)[0, 0]

    def at_first(arrays):
        return [(array, 0) for array in arrays]

    def of(lists, t):
        return [array for u in units if kinds[u] == t for array in lists[u]]

    def to_owners(products):
        return [shift_seq(p.astype(BF16), -k) for k, p in enumerate(products, 1)]

    def text_members(products):
        return jnp.split(products.reshape(-1, padded, width), members, axis=0)

    active, hidden_grad = [None] * len(units), [None] * len(units)
    came_mid = [None] * len(units)
    own_text = {}

    def feed(u):
        t = kinds[u]
        normed_mid[u] = order(*normed_mid[u])
        if t == 1:
            normed_mid[u] = [jnp.concatenate(normed_mid[u], axis=0).reshape(1, -1, width)]
        active[u], hidden_grad[u] = feed_forward(
            at_first(normed_mid[u]), mlp_pieces[u], w_fc1, w_fc2, t
        )
        if t == 0:
            products = [times_t(values, w_fc1[t]).astype(BF16) for values in hidden_grad[u][1:]]
            order.mark(*products)
        else:
            parts = text_members(times_t(hidden_grad[u][0], w_fc1[t]))
            own_text["mid"], products = parts[0], parts[1:]
            order.mark(parts[0])
        came_mid[u] = to_owners(products)

    for u in [*both, text]:
        normed_mid[u] = order(*normed_mid[u])
    order.mark(*[values for u in units for values in normed_mid[u][1:]])
    feed(text)
    ready = order(active[text][0], hidden_grad[text][0])
    fc2_txt = scattered(at_first(ready[:1]), mlp_pieces[text])
    fc1_txt = scattered(at_first(normed_mid[text]), at_first(ready[1:]))
    for s in both:
        feed(s)
    active[0][0] = order(active[0][0])[0]
    fc2_img = scattered(
        at_first(of(active, 0)), [p for u in units if kinds[u] == 0 for p in mlp_pieces[u]]
    )

    middle_grad, late_grads, head_grads, branch_grad = {}, {}, {}, {}
    grads_now = own_grad()
    for u in [0, text, *range(1, sequences)]:
        t = kinds[u]
        came = order(*came_mid[u])
        if t == 0:
            mid_grad = times_t(hidden_grad[u][0], w_fc1[t])
        else:
            mid_grad = own_text["mid"]
        for values in came:
            mid_grad = mid_grad + values.astype(F32)
        average, root = mid_stats[u]
        unit = (middle[u] - average) * root
        scale_mlp_grad = jnp.sum(mid_grad * unit, axis=1)
        shift_mlp_grad = jnp.sum(mid_grad, axis=1)
        total = grads_now[u] + norm_back(mid_grad * (1.0 + vectors[u][4]), unit, root)
        middle_grad[u] = total
        gate_attn_grad = jnp.sum(total * branch[u], axis=1)
        late_grads[u] = [gate_attn_grad, shift_mlp_grad, scale_mlp_grad]
        branch_grad[u] = (vectors[u][2] * total).astype(BF16)
        attended_grad = times_t(branch_grad[u], w_proj[t]).astype(BF16)
        attended_grad = jnp.roll(attended_grad, -member * head_width, axis=-1)
        parts = []
        for k in every:
            part = attended_grad[..., k * head_width : (k + 1) * head_width]
            if head_padded > head_width:
                part = jnp.pad(part, ((0, 0), (0, 0), (0, head_padded - head_width)))
            parts.append(part)
        order.mark(*parts)
        head_grads[u] = [shift_seq(part, k) if k else part for k, part in enumerate(parts)]
    ready = order(branch_grad[text], branch_grad[0])
    branch_grad[text], branch_grad[0] = ready
    halves = None
    for t in range(2):
        halves = weight_sum(
            at_first([own_attended[u].reshape(1, -1, width) for u in units if kinds[u] == t]),
            at_first([branch_grad[u].reshape(1, -1, width) for u in units if kinds[u] == t]),
            shards,
            before=halves,
            place=t,
            places=2,
        )
    order.mark(*halves)
    proj_both = lax.psum_scatter(halves[0], "fsdp", scatter_dimension=0, tiled=True)[0]
    hidden_grad[0][0] = order(hidden_grad[0][0])[0]
    fc1_img = reduction(at_first(of(normed_mid, 0)), at_first(of(hidden_grad, 0)))
    advance([], [fc1_img])
    grads = [
        [head_grads[s][k] for k in every] + [head_grads[text][k][s : s + 1] for k in every]
        for s in both
    ]
    def finish(reds):
        while reds:
            advance(reds, reds)
            reds = [red for red in reds if red.bit < shards]

    def send_rows(values):
        blocks = values.reshape((members, -1) + values.shape[1:])
        own = pick(blocks, member, 0)
        parts = [pick(blocks, (member + k) % members, 0) for k in range(1, members)]
        order.mark(own, *parts)
        return [own] + [shift_seq(part, k) for k, part in enumerate(parts, 1)]

    def by_place(parts):
        stacked = jnp.stack(parts)
        return [pick(stacked, (member - i) % members, 0) for i in every]

    gain_parts, raw_grads, came_in, came_mlp = [], [], [], []
    for u in units:
        values = order(*active[u])
        active[u] = values
        if kinds[u] == 0:
            products = [times(v, w_fc2[0]).astype(BF16) for v in values[1:]]
            order.mark(*products)
        else:
            parts = text_members(times(values[0], w_fc2[1]))
            own_text["mlp"], products = parts[0], parts[1:]
            order.mark(parts[0])
        came_mlp.append(to_owners(products))
    advance([fc1_img], [fc1_img])

    def in_products(s):
        values = order(*raw_grads[s][1:members])
        products = [times_t(v, w_qkv[0]).astype(BF16) for v in values]
        order.mark(*products)
        return to_owners(products)

    for s in both:
        before = None
        for group in range(groups):
            before, gain_part = attend_back(
                raw[s],
                grads[s],
                attended[s],
                norms[s],
                order(gains)[0],
                live_lanes,
                s,
                img_total,
                groups,
                group,
                before,
            )
            gain_parts.append(gain_part)
            order.mark(gain_part)
            if (s, group) in ((sequences - 1, 0), (sequences - 1, groups - 1)):
                advance([fc1_img], [fc1_img])
            if (s, group) == (sequences - 1, 0):
                came_mlp = [order(*came) for came in came_mlp]
                order.mark(*[values for came in came_mlp for values in came])
            if (s, group) == (sequences - 1, 0):
                fc1_txt = send_rows(order(fc1_txt)[0].astype(F32))
        raw_grads.append(before)
        if s == 0:
            advance([fc1_img], [fc1_img])
        if s < sequences - 1:
            came_in.append(in_products(s))
    came_in = [order(*came) for came in came_in]
    fc2_img, fc2_txt = order(fc2_img, fc2_txt)
    fc1_txt = [fc1_txt[0], *order(*fc1_txt[1:])]
    order.mark(fc2_img, fc2_txt)
    order.mark(*[values for came in came_in for values in came], *fc1_txt)
    values = order(*raw_grads[-1][:members])
    raw_grads[-1] = [*values, *raw_grads[-1][members:]]
    qkv_img = reduction(
        [(normed_img[k], s) for s in both for k in every],
        at_first([raw_grads[s][k] for s in both for k in every]),
    )
    advance([], [qkv_img])
    came_in.append(in_products(sequences - 1))
    advance([qkv_img], [qkv_img])
    raw_text = jnp.concatenate([raw_grads[s][members + k] for k in every for s in both], axis=0)
    raw_text = order(raw_text)[0]
    qkv_txt = reduction(
        at_first([normed_txt.reshape(1, -1, width)]), at_first([raw_text.reshape(1, -1, triple)])
    )
    advance([], [qkv_txt])
    raw_text = order(raw_text)[0]
    parts = text_members(times_t(raw_text, w_qkv[1]))
    own_text["in"] = parts[0]
    came_in.append(to_owners(parts[1:]))
    order.mark(parts[0])
    in_grads, in_sums, outs, gate_sums = {}, {}, {}, {}
    tokens = own_in()

    def input_back(u):
        came = order(*came_in[u])
        in_grad = times_t(raw_grads[u][0], w_qkv[0]) if kinds[u] == 0 else own_text["in"]
        for values in came:
            in_grad = in_grad + values.astype(F32)
        average, root = statistics(tokens[u])
        unit = (tokens[u] - average) * root
        in_sums[u] = [jnp.sum(in_grad, axis=1), jnp.sum(in_grad * unit, axis=1)]
        in_grads[u] = middle_grad[u] + norm_back(in_grad * (1.0 + vectors[u][1]), unit, root)
        order.mark(in_grads[u], *in_sums[u])

    def output(u):
        came = order(*came_mlp[u])
        mlp_out = times(active[u][0], w_fc2[0]) if kinds[u] == 0 else own_text["mlp"]
        for values in came:
            mlp_out = mlp_out + values.astype(F32)
        result = middle[u] + vectors[u][5] * mlp_out
        if kinds[u] == 1:
            result = result * text_rows
        outs[u] = result.astype(BF16)
        gate_sums[u] = jnp.sum(grads_late[u] * mlp_out, axis=1)
        order.mark(outs[u], gate_sums[u])

    grads_late = own_grad()
    output(0)
    advance([qkv_txt], [qkv_txt])
    proj_both = order(proj_both)[0]
    order.mark(proj_both)
    advance([qkv_img], [qkv_img])
    input_back(sequences - 1)
    advance([qkv_img], [qkv_img])
    input_back(text)
    for s in range(sequences - 1):
        input_back(s)
    advance([qkv_txt], [qkv_txt])
    for u in units:
        if u:
            output(u)
    mod_rows = [
        jnp.concatenate([*in_sums[u], *late_grads[u], gate_sums[u]], axis=-1) for u in units
    ]
    img_out = jnp.concatenate([outs[s] for s in both], axis=0)
    txt_out = outs[text][:, :slots]
    img_grad = jnp.concatenate([in_grads[s] for s in both], axis=0)
    txt_grad = in_grads[text][:, :slots]

    gain_own = sum(jnp.sum(part, axis=0) for part in gain_parts)[:4]
    gain_own = (gain_own[:, :HEAD] + gain_own[:, HEAD:]).reshape(-1)
    mod_own = jnp.stack([jnp.concatenate(mod_rows[:-1], axis=0), mod_rows[-1]], axis=1)
    mod_count = mod_own.size
    own_shared = jnp.concatenate([mod_own.reshape(-1), gain_own])
    order.mark(own_shared)
    came_shared = gather_seq(own_shared)[1:]
    finish([fc1_img])
    finish([qkv_img])
    ready = order(fc2_img, fc2_txt)
    order.mark(*ready)
    qkv_rows = send_rows(qkv_img.result()[0])
    shared = sum(order(*came_shared), own_shared)
    gain_high = shared[mod_count:].astype(BF16)
    gain_low = (shared[mod_count:] - gain_high.astype(F32)).astype(BF16)
    packed = jnp.concatenate([shared[:mod_count].astype(BF16), gain_high, gain_low])
    packed = jnp.broadcast_to(packed.reshape(1, -1, LANES), (shards, packed.size // LANES, LANES))
    order.mark(packed)
    packed = lax.all_to_all(packed, "fsdp", split_axis=0, concat_axis=0, tiled=True)
    advance([qkv_txt], [qkv_txt])

    ready = order(*ready)
    fc2_grad = jnp.stack(ready[:2]).astype(F32)
    fc1_rows = send_rows(fc1_img.result()[0])
    proj_rows = send_rows(jnp.transpose(proj_both.astype(F32), (1, 0, 2)))

    def heads_apart(parts):
        parts = by_place(parts)
        return jnp.concatenate(
            [
                parts[m][:, (g * 3 + part) * group_width :][
                    :, : min(group_width, head_width - g * group_width)
                ]
                for part in range(3)
                for m in every
                for g in range(groups)
            ],
            axis=1,
        )

    qkv_rows = [qkv_rows[0], *order(*qkv_rows[1:])]
    image_grad = heads_apart(qkv_rows)
    order.mark(image_grad, fc2_grad)

    packed = order(packed)[0]
    mod_lanes = mod_count // LANES
    every_mod = packed[:, :mod_lanes].reshape(shards * sequences, 2, mod_width)
    gain_grad = jnp.sum(packed[:, mod_lanes:].astype(F32), axis=0)
    gain_grad = gain_grad.reshape(2, 2, 2 * HEAD).sum(axis=0)
    cond_part = jnp.einsum("stm,tdm->sd", every_mod, ada_w, preferred_element_type=F32)
    order.mark(cond_part)
    cond_full = lax.all_to_all(cond_part, "fsdp", split_axis=0, concat_axis=1, tiled=True)
    finish([qkv_txt])
    text_rows_sent = send_rows(qkv_txt.result()[0])
    every_mod = order(every_mod)[0]
    out_rows = width // (shards * members)
    own_cols = lax.dynamic_slice_in_dim(cond_cols, member * out_rows, out_rows, 1)
    ada_grad = jnp.einsum("sr,stm->trm", own_cols, every_mod, preferred_element_type=F32)
    proj_grad = jnp.transpose(sum(order(*proj_rows[1:]), proj_rows[0]), (1, 0, 2))
    fc1_rows = [fc1_rows[0], *order(*fc1_rows[1:])]
    fc1_grad = jnp.stack([join_units(by_place(rows), shards) for rows in (fc1_rows, fc1_txt)])
    order.mark(ada_grad, proj_grad, fc1_grad)
    cond_grad = jax.vjp(jax.nn.silu, cond.astype(F32))[1](order(cond_full)[0])[0]
    text_grad = heads_apart([text_rows_sent[0], *order(*text_rows_sent[1:])])
    qkv_grad = jnp.stack([image_grad, text_grad])
    return (
        img_out,
        txt_out,
        img_grad,
        txt_grad,
        cond_grad,
        ada_grad,
        qkv_grad,
        proj_grad,
        fc1_grad,
        fc2_grad,
        gain_grad,
    )


def solution(mesh):
    tokens, rows = P("fsdp", "seq", None), P("fsdp", None)
    weight, weight_grad = P(None, "fsdp", None), P(None, ("fsdp", "seq"), None)
    in_specs = (tokens, tokens, rows, rows) + (weight,) * 5 + (P(), tokens, tokens)
    out_specs = (tokens,) * 4 + (rows,) + (weight_grad,) * 5 + (P(),)
    return jax.shard_map(body, mesh=mesh, in_specs=in_specs, out_specs=out_specs, check_vma=False)
```
